512 devices in a mesh: dp: 32 (over z, x), expert: 16 (over y, core).
Axes of the slice: x: 4, y: 8, z: 8, core: 2. Of those that a mesh axis runs over, the one named last changes fastest.
Arguments:
- tokens: bfloat16 [16384, 2048], P(('dp', 'expert')), may hold values from -6 to 6
- d_out: bfloat16 [16384, 2048], P(('dp', 'expert')), may hold values from -6 to 6
- expert_ids: int32 [16384, 4], P(('dp', 'expert')), may hold values from 0 to 127, all different within a row; in each aligned block of 32 rows (0 to 31, 32 to 63, ...) at most 2 rows name the same one
- gate_weights: float32 [16384, 4], P(('dp', 'expert')), may hold values from 0.05 to 1
- w_in: bfloat16 [512, 2048, 256], P(('dp', 'expert')), may hold values from -0.125 to 0.125
- w_out: bfloat16 [512, 256, 2048], P(('dp', 'expert')), may hold values from -0.1875 to 0.1875
Outputs:
- d_tokens: bfloat16 [16384, 2048], P(('dp', 'expert'))
- d_gates: float32 [16384, 4], P(('dp', 'expert'))
- d_w_in: bfloat16 [512, 2048, 256], P(('dp', 'expert'))
- d_w_out: bfloat16 [512, 256, 2048], P(('dp', 'expert'))
The draws below stay inside these ranges and needn't reach their ends.
Inputs may be any that keep to these rules, and one draw needn't show every extreme that they name: `expert_ids`: each token names 4 different experts. Among the 32 tokens of one device no expert is named more than 2 times, and in every draw some device names some expert exactly 2 times.
All inputs are finite; a program needn't handle non-finite values.
Results may differ from the reference program's by a relative error of at most 0.02.
Values may be sent and summed in bfloat16 or wider, within the bound.
No kernel may reach another device: no remote copies, remote signals or barrier semaphores. Data moves between devices by JAX's collectives and lax.ppermute only.
A program may use at most 128 MiB of HBM per device.

```python
import math
import jax
import jax.numpy as jnp
import numpy as np
from jax import lax

D = 2048
H = 1024
TOPK = 4
SPLIT = 4
TOK_DEV = 32
EXPERTS = 128
CAP = 2
TOKENS = 16384
SHARDS = 512
N_DP = 32
N_EXPERT = 16


def block_levels(own_key, dims, pieces, least, top_value):
    def one(axis_at, shards_of):
        heights = jax.random.uniform(jax.random.fold_in(jax.random.fold_in(own_key, 6), axis_at), (shards_of,), jnp.float32, least / len(pieces), top_value / len(pieces))
        return jnp.repeat(jnp.exp(heights), dims[axis_at] // shards_of).reshape((-1,) + (1,) * (len(dims) - axis_at - 1))

    factor_of = one(*pieces[0])
    for cut in pieces[1:]:
        factor_of = factor_of * one(*cut)
    return factor_of


def routed_block(stream_key, own, number, rows, number_of, top, bound, skew):
    sequence = jax.random.permutation(stream_key, number_of)
    packed, ordinary = portions_of(number_of, rows * top, bound, skew, True), portions_of(number_of, rows * top, bound, skew, False)
    places = jnp.arange(number_of)

    def named(lengths, rotation):
        used = int((lengths > 0).sum())
        fixed = max(1, used // 4)
        passed = fixed + (places - fixed + rotation * (used - fixed)) % max(1, number_of - fixed)
        return jnp.zeros((number_of,), jnp.int32).at[sequence[jnp.where(places < fixed, places, passed)]].set(jnp.asarray(lengths, jnp.int32))

    lengths = jnp.where(number % 4 == 0, named(packed, number // 4), named(ordinary, number - number // 4 - 1))
    mixed = jax.random.permutation(jax.random.fold_in(own, 3), number_of)
    giver, taker = mixed[0:number_of // 2 * 2:2], mixed[1:number_of // 2 * 2:2]
    slack = jnp.minimum(lengths[giver] - 1, bound - lengths[taker]) // 2
    slack = jnp.where((giver == sequence[0]) | (taker == sequence[0]) | (lengths[taker] == 0), 0, jnp.maximum(slack, 0))
    passed = jax.random.randint(jax.random.fold_in(own, 4), (number_of // 2,), 0, 1 << 20) % (slack + 1)
    lengths = lengths.at[giver].add(-passed).at[taker].add(passed)
    members = jnp.searchsorted(jnp.cumsum(lengths), jnp.arange(rows * top), side="right").astype(jnp.int32)
    listing = members.reshape(top, rows).T
    listing = listing[jax.random.permutation(jax.random.fold_in(own, 1), rows)]
    rotation = jax.random.randint(jax.random.fold_in(own, 2), (rows, 1), 0, top)
    return jnp.take_along_axis(listing, (jnp.arange(top)[None, :] + rotation) % top, axis=1)


def portions_of(count, total, reach, skew, full):
    loads = [(1 << 20) // math.isqrt(grade ** skew) + 1 for grade in range(1, count + 1)]
    largest = reach if full else min(reach, max(-(-total // count), total * loads[0] // sum(loads)))
    least = 1 if total - largest >= count - 1 else 0
    holding, spare = [largest] + [least] * (count - 1), total - largest - least * (count - 1)
    while spare > 0:
        free = [i for i in range(1, count) if holding[i] < largest] or [i for i in range(1, count) if holding[i] < reach]
        pool, budget = sum([loads[i] for i in free]), spare
        for i in free:
            extra = min(reach - holding[i], max(1, budget * loads[i] // pool), spare)
            holding[i] = holding[i] + extra
            spare = spare - extra
    return np.array(holding)


def noise(key, shape, spread, most, split=(), held_as=jnp.bfloat16):
    values = jax.random.normal(key, shape, jnp.float32) * spread
    if len(split) > 0:
        values = block_levels(key, shape, split, -0.22, 0.18) * values
    return jnp.clip(values, min=-most, max=most).astype(held_as)


def setup_inputs(seed: int = 0) -> dict:
    key_list = jax.random.split(jax.random.key(seed), 7)
    tokens = noise(key_list[0], (TOKENS, D), 1.0, 6.0, ((0, 512),))
    d_out = noise(key_list[1], (TOKENS, D), 1.0, 6.0, ((0, 512),))
    expert_ids_keys = jax.random.split(jax.random.fold_in(key_list[2], 1), TOKENS // TOK_DEV)
    expert_ids_turns = jax.random.permutation(jax.random.fold_in(key_list[2], 3), TOKENS // TOK_DEV)
    expert_ids = jax.vmap(lambda own, number: routed_block(jax.random.fold_in(key_list[2], 2), own, number, TOK_DEV, EXPERTS, TOPK, CAP, 2))(expert_ids_keys, expert_ids_turns).reshape((TOKENS, TOPK))
    gate_weights = jnp.clip(jnp.exp(math.log(1.0) - 2.9957323 * jax.random.uniform(key_list[3], (TOKENS, TOPK), jnp.float32) ** block_levels(key_list[3], (TOKENS, TOPK), ((0, 512),), -0.2, 0.2)), 0.05, 1.0)
    w_in = noise(key_list[4], (SHARDS, D, H // SPLIT), D ** -0.5, 0.125, ((0, 512),))
    w_out = noise(key_list[5], (SHARDS, H // SPLIT, D), H ** -0.5, 0.1875, ((0, 512),))
    return {"tokens": tokens, "d_out": d_out, "expert_ids": expert_ids, "gate_weights": gate_weights, "w_in": w_in, "w_out": w_out}


def reference(tokens, d_out, expert_ids, gate_weights, w_in, w_out):
    flat_ids = expert_ids.reshape(-1)
    flat_gates = gate_weights.reshape(-1)
    most_rows = N_DP * N_EXPERT * CAP

    def per_expert(carry, expert):
        d_tok, d_gate = carry
        hits = flat_ids == expert
        picked = jnp.nonzero(hits, size=most_rows, fill_value=0)[0].astype(jnp.int32)
        valid = jnp.arange(most_rows) < jnp.sum(hits.astype(jnp.int32))
        token_of = picked // TOPK
        rows_in = jnp.where(valid[:, None], tokens[token_of], 0).astype(jnp.float32)
        rows_grad = jnp.where(valid[:, None], d_out[token_of], 0).astype(jnp.float32)
        gate_rows = jnp.where(valid, flat_gates[picked], 0.0).astype(jnp.float32)
        start = (expert * SPLIT).astype(jnp.int32)
        w_first = lax.dynamic_slice_in_dim(w_in, start, SPLIT, 0).astype(jnp.float32)
        w_second = lax.dynamic_slice_in_dim(w_out, start, SPLIT, 0).astype(jnp.float32)
        preact = jnp.einsum("rd,qdh->qrh", rows_in, w_first)
        sigmas = jax.nn.sigmoid(preact)
        activated = preact * sigmas
        pulled = jnp.einsum("rd,qhd->qrh", rows_grad, w_second)
        gate_col = gate_rows[None, :, None]
        d_preact = (gate_col * pulled * sigmas * (1.0 + preact * (1.0 - sigmas))).astype(jnp.bfloat16)
        partial_dx = jnp.einsum("qrh,qdh->qrd", d_preact.astype(jnp.float32), w_first).astype(jnp.bfloat16)
        rows_dx = jnp.sum(partial_dx.astype(jnp.float32), axis=0)
        gate_sum = jnp.sum(activated * pulled, axis=(0, 2))
        scaled_act = (gate_col * activated).astype(jnp.bfloat16)
        grad_first = jnp.einsum("rd,qrh->qdh", rows_in, d_preact.astype(jnp.float32)).astype(jnp.bfloat16)
        grad_second = jnp.einsum("qrh,rd->qhd", scaled_act.astype(jnp.float32), rows_grad).astype(jnp.bfloat16)
        d_tok = d_tok.at[token_of].add(rows_dx)
        d_gate = d_gate.at[picked].add(jnp.where(valid, gate_sum, 0.0))
        return (d_tok, d_gate), (grad_first, grad_second)

    start_carry = (jnp.zeros(tokens.shape, jnp.float32), jnp.zeros(flat_gates.shape, jnp.float32))
    (d_tok, d_gate), (grads_first, grads_second) = lax.scan(per_expert, start_carry, jnp.arange(EXPERTS, dtype=jnp.int32))
    d_w_in = grads_first.reshape(w_in.shape)
    d_w_out = grads_second.reshape(w_out.shape)
    return (d_tok.astype(jnp.bfloat16), d_gate.reshape(gate_weights.shape), d_w_in, d_w_out)
```

```python
import jax
import jax.numpy as jnp
import numpy as np
from jax import lax
from jax.experimental import pallas as pl
from jax.experimental.pallas import tpu as pltpu
from jax.sharding import Mesh
from jax.sharding import PartitionSpec as P

TOPK = 4
LANES = 128
AXES = ("dp", "yh", "yl", "core")
ROUTE = ("dp", "yh")
GATE_ROWS = 8
HOLD_FLOPS = int(3e10)
SWAP = [(0, 1), (1, 0)]
f32, bf16 = jnp.float32, jnp.bfloat16


def dispatch_kernel(ids_ref, gates_ref, tok_ref, dout_ref, out_ref, target_ref, count_ref):
    tokens, width = tok_ref.shape[0], tok_ref.shape[1]
    out_ref[...] = jnp.zeros_like(out_ref)

    def clear(i, carry):
        count_ref[i] = 0
        return carry

    lax.fori_loop(0, count_ref.shape[0], clear, 0, unroll=8)

    def place(t, carry):
        row = tok_ref[t]
        grad = dout_ref[t].astype(f32)
        for k in range(TOPK):
            e = ids_ref[t, k]
            slot = count_ref[e]
            count_ref[e] = slot + 1
            at = 2 * e + slot
            target_ref[t, k] = at
            out_ref[at, 0:width, :] = row
            out_ref[at, width : 2 * width, :] = (grad * gates_ref[t, k]).astype(bf16)
        return carry

    lax.fori_loop(0, tokens, place, 0)


def dispatch(ids, gates, tok3, dout3, experts):
    tokens, width, _ = tok3.shape
    smem = pl.BlockSpec(memory_space=pltpu.SMEM)
    vmem = pl.BlockSpec(memory_space=pltpu.VMEM)
    return pl.pallas_call(
        dispatch_kernel,
        out_shape=(
            jax.ShapeDtypeStruct((2 * experts, 2 * width, LANES), bf16),
            jax.ShapeDtypeStruct((tokens, TOPK), jnp.int32),
        ),
        in_specs=[smem, smem, vmem, vmem],
        out_specs=(vmem, smem),
        scratch_shapes=[pltpu.SMEM((experts,), jnp.int32)],
        name="dispatch",
    )(ids, gates, tok3, dout3)


def hold(x, flops):
    anywhere = pl.BlockSpec(memory_space=pl.ANY)
    return pl.pallas_call(
        lambda x_ref, y_ref: None,
        out_shape=jax.ShapeDtypeStruct(x.shape, x.dtype),
        in_specs=[anywhere],
        out_specs=anywhere,
        input_output_aliases={0: 0},
        cost_estimate=pl.CostEstimate(flops=flops, bytes_accessed=0, transcendentals=0),
        name="hold",
    )(x)


def combine_kernel(target_ref, back_ref, dx_ref, gate_ref):
    tokens, width = dx_ref.shape[0], dx_ref.shape[1]
    lane = lax.broadcasted_iota(jnp.int32, (1, LANES), 1)

    def total(t, carry):
        acc = jnp.zeros((width, LANES), f32)
        gate = jnp.zeros((1, LANES), f32)
        for k in range(TOPK):
            at = target_ref[t, k]
            e, slot = lax.shift_right_logical(at, 1), lax.bitwise_and(at, 1)
            first = pl.multiple_of(slot * width, width)
            acc += back_ref[e, pl.ds(first, width), :].astype(f32)
            extra = back_ref[e, 2 * width : 2 * width + GATE_ROWS, :].astype(f32)
            pair = jnp.where(slot == 0, extra[0:2, :], extra[2:4, :])
            gate = jnp.where(lane == k, pair[0:1, :] + pair[1:2, :], gate)
        dx_ref[t] = acc.astype(bf16)
        gate_ref[pl.ds(t, 1), :] = gate
        return carry

    lax.fori_loop(0, tokens, total, 0)


def combine(target, back, tokens, width):
    vmem = pl.BlockSpec(memory_space=pltpu.VMEM)
    return pl.pallas_call(
        combine_kernel,
        out_shape=(
            jax.ShapeDtypeStruct((tokens, width, LANES), bf16),
            jax.ShapeDtypeStruct((tokens, LANES), f32),
        ),
        in_specs=[pl.BlockSpec(memory_space=pltpu.SMEM), vmem],
        out_specs=(vmem, vmem),
        name="combine",
    )(target, back)


def dot(a, b, ca, cb):
    return lax.dot_general(a, b, (((ca,), (cb,)), ((), ())), preferred_element_type=f32)


def on_device(tokens, d_out, expert_ids, gate_weights, w_in, w_out):
    tok_rows, model = tokens.shape
    width = model // LANES
    experts = lax.axis_size("dp") * lax.axis_size("yh")
    slots = 2 * experts
    own_in, own_out = w_in[0], w_out[0]
    hidden = own_out.shape[0]
    oth = lax.ppermute(jnp.concatenate([own_in.T, own_out], axis=0), "yl", SWAP)
    outgoing, target = dispatch(
        expert_ids,
        gate_weights,
        tokens.reshape(tok_rows, width, LANES),
        d_out.reshape(tok_rows, width, LANES),
        experts,
    )
    outgoing = outgoing.reshape(experts, 4 * width, LANES)
    arrived = lax.all_to_all(outgoing, ROUTE, split_axis=0, concat_axis=0, tiled=True)
    arrived, oth = lax.optimization_barrier((arrived, hold(oth, HOLD_FLOPS)))
    oth_in, oth_out = oth[:hidden], oth[hidden:]
    mine = arrived.reshape(slots, 2 * model)
    theirs = lax.ppermute(mine, "core", SWAP)
    rows = jnp.concatenate([mine, theirs], axis=0)
    rows_x, rows_g = rows[:, :model], rows[:, model:]

    def quarter(first, second, depth):
        preact = dot(rows_x, first, 1, depth)
        pulled = dot(rows_g, second, 1, 1)
        sig = jax.nn.sigmoid(preact)
        act = preact * sig
        d_pre = (pulled * sig * (1.0 + preact * (1.0 - sig))).astype(bf16)
        gate = jnp.sum(act * pulled, axis=1, keepdims=True)
        return d_pre, act.astype(bf16), gate

    dp_own, act_own, gate_own = quarter(own_in, own_out, 0)
    dp_oth, act_oth, gate_oth = quarter(oth_in, oth_out, 1)
    far = jnp.concatenate([dot(dp_oth, rows_x, 0, 0), dot(act_oth, rows_g, 0, 0)], axis=0).astype(bf16)
    came = lax.ppermute(far, "yl", SWAP)
    dx = dot(dp_own, own_in, 1, 1) + dot(dp_oth, oth_in, 1, 0)
    gate = gate_own + gate_oth
    dx_peer = lax.ppermute(dx[slots:].astype(bf16), "core", SWAP)
    gate_peer = lax.ppermute(gate[slots:], "core", SWAP)
    dx_sum = (dx[:slots] + dx_peer.astype(f32)).astype(bf16)
    gate_sum = gate[:slots] + gate_peer
    gate_high = gate_sum.astype(bf16)
    gate_low = (gate_sum - gate_high.astype(f32)).astype(bf16)
    gate_rows = jnp.concatenate([gate_high, gate_low], axis=1).reshape(experts, 4, 1)
    gate_rows = jnp.pad(gate_rows, ((0, 0), (0, GATE_ROWS - 4), (0, 0)))
    gate_rows = jnp.broadcast_to(gate_rows, (experts, GATE_ROWS, LANES))
    back = jnp.concatenate([dx_sum.reshape(experts, 2 * width, LANES), gate_rows], axis=1)
    returned = lax.all_to_all(back, ROUTE, split_axis=0, concat_axis=0, tiled=True)
    d_tok3, gate_rows = combine(target, returned, tok_rows, width)
    d_gates = gate_rows[:, :TOPK] / gate_weights
    d_first = (dot(rows_x, dp_own, 0, 0) + came[:hidden].T.astype(f32)).astype(bf16)
    d_second = (dot(act_own, rows_g, 0, 0) + came[hidden:].astype(f32)).astype(bf16)
    return (d_tok3.reshape(tok_rows, model), d_gates, d_first[None], d_second[None])


def solution(mesh):
    dp, expert = mesh.devices.shape
    fine = Mesh(np.asarray(mesh.devices).reshape(dp, expert // 4, 2, 2), AXES)
    flat, block = P(AXES, None), P(AXES, None, None)
    return jax.shard_map(
        on_device,
        mesh=fine,
        in_specs=(flat, flat, flat, flat, block, block),
        out_specs=(flat, flat, block, block),
        check_vma=False,
    )
```

```python
import functools

import jax
import jax.numpy as jnp
import numpy as np
from jax import lax
from jax.experimental import pallas as pl
from jax.experimental.pallas import tpu as pltpu
from jax.sharding import Mesh
from jax.sharding import PartitionSpec as P

TOPK = 4
LANES = 128
AXES = ("dp", "yh", "yl", "core")
GATE_ROWS = 8
HOLD_FLOPS = int(3e10)
SWAP = [(0, 1), (1, 0)]
f32, bf16 = jnp.float32, jnp.bfloat16


def dispatch_kernel(ids_ref, gates_ref, tok_ref, dout_ref, out_ref, target_ref, count_ref):
    tokens, width = tok_ref.shape[0], tok_ref.shape[1]
    out_ref[...] = jnp.zeros_like(out_ref)

    def clear(i, carry):
        count_ref[i] = 0
        return carry

    lax.fori_loop(0, count_ref.shape[0], clear, 0, unroll=8)

    def place(t, carry):
        row = tok_ref[t]
        grad = dout_ref[t].astype(f32)
        for k in range(TOPK):
            e = ids_ref[t, k]
            slot = count_ref[e]
            count_ref[e] = slot + 1
            at = 2 * e + slot
            target_ref[t, k] = at
            out_ref[at, 0:width, :] = row
            out_ref[at, width : 2 * width, :] = (grad * gates_ref[t, k]).astype(bf16)
        return carry

    lax.fori_loop(0, tokens, place, 0)


def dispatch(ids, gates, tok3, dout3, experts):
    tokens, width, _ = tok3.shape
    smem = pl.BlockSpec(memory_space=pltpu.SMEM)
    vmem = pl.BlockSpec(memory_space=pltpu.VMEM)
    return pl.pallas_call(
        dispatch_kernel,
        out_shape=(
            jax.ShapeDtypeStruct((2 * experts, 2 * width, LANES), bf16),
            jax.ShapeDtypeStruct((tokens, TOPK), jnp.int32),
        ),
        in_specs=[smem, smem, vmem, vmem],
        out_specs=(vmem, smem),
        scratch_shapes=[pltpu.SMEM((experts,), jnp.int32)],
        name="dispatch",
    )(ids, gates, tok3, dout3)


def hold(x, flops):
    anywhere = pl.BlockSpec(memory_space=pl.ANY)
    return pl.pallas_call(
        lambda x_ref, y_ref: None,
        out_shape=jax.ShapeDtypeStruct(x.shape, x.dtype),
        in_specs=[anywhere],
        out_specs=anywhere,
        input_output_aliases={0: 0},
        cost_estimate=pl.CostEstimate(flops=flops, bytes_accessed=0, transcendentals=0),
        name="hold",
    )(x)


def combine_kernel(target_ref, back_ref, dx_ref, gate_ref):
    tokens, width = dx_ref.shape[0], dx_ref.shape[1]
    lane = lax.broadcasted_iota(jnp.int32, (1, LANES), 1)

    def total(t, carry):
        acc = jnp.zeros((width, LANES), f32)
        gate = jnp.zeros((1, LANES), f32)
        for k in range(TOPK):
            at = target_ref[t, k]
            e, slot = lax.shift_right_logical(at, 1), lax.bitwise_and(at, 1)
            first = pl.multiple_of(slot * width, width)
            acc += back_ref[e, pl.ds(first, width), :].astype(f32)
            extra = back_ref[e, 2 * width : 2 * width + GATE_ROWS, :].astype(f32)
            pair = jnp.where(slot == 0, extra[0:2, :], extra[2:4, :])
            gate = jnp.where(lane == k, pair[0:1, :] + pair[1:2, :], gate)
        dx_ref[t] = acc.astype(bf16)
        gate_ref[pl.ds(t, 1), :] = gate
        return carry

    lax.fori_loop(0, tokens, total, 0)


def combine(target, back, tokens, width):
    vmem = pl.BlockSpec(memory_space=pltpu.VMEM)
    return pl.pallas_call(
        combine_kernel,
        out_shape=(
            jax.ShapeDtypeStruct((tokens, width, LANES), bf16),
            jax.ShapeDtypeStruct((tokens, LANES), f32),
        ),
        in_specs=[pl.BlockSpec(memory_space=pltpu.SMEM), vmem],
        out_specs=(vmem, vmem),
        name="combine",
    )(target, back)


def dot(a, b, ca, cb):
    return lax.dot_general(a, b, (((ca,), (cb,)), ((), ())), preferred_element_type=f32)


def experts_kernel(
    rows_hbm, w0, w1, w2, w3, g0, g1, g2, g3, dx_ref, gate_ref, rows, weights, grads, total, in_sems, out_sems
):
    hidden, model = weights.shape[1] // 2, weights.shape[2]
    loads = [pltpu.make_async_copy(rows_hbm, rows, in_sems.at[4])]
    loads += [
        pltpu.make_async_copy(w, weights.at[q], in_sems.at[q])
        for q, w in enumerate((w0, w1, w2, w3))
    ]
    stores = [
        pltpu.make_async_copy(grads.at[q], g, out_sems.at[q])
        for q, g in enumerate((g0, g1, g2, g3))
    ]
    for load in loads:
        load.start()
    loads[0].wait()
    gate = jnp.zeros((rows.shape[0], 1), f32)
    for q in range(4):
        loads[1 + q].wait()
        preact = dot(rows[:, :model], weights[q, :hidden, :], 1, 1)
        pulled = dot(rows[:, model:], weights[q, hidden:, :], 1, 1)
        sig = jax.nn.sigmoid(preact)
        act = preact * sig
        d_pre = (pulled * sig * (1.0 + preact * (1.0 - sig))).astype(bf16)
        gate += jnp.sum(act * pulled, axis=1, keepdims=True)
        act = act.astype(bf16)
        grads[q, :hidden, :] = dot(d_pre, rows[:, :model], 0, 0).astype(bf16)
        grads[q, hidden:, :] = dot(act, rows[:, model:], 0, 0).astype(bf16)
        stores[q].start()
        part = dot(d_pre, weights[q, :hidden, :], 1, 0)
        if q < 3:
            total[...] = part if q == 0 else total[...] + part
        else:
            dx_ref[...] = (total[...] + part).astype(bf16)
    gate_ref[...] = jnp.broadcast_to(gate, gate_ref.shape)
    for store in stores:
        store.wait()


def run_experts(rows, blocks):
    slots, model = rows.shape[0], rows.shape[1] // 2
    anywhere = pl.BlockSpec(memory_space=pl.ANY)
    vmem = pl.BlockSpec(memory_space=pltpu.VMEM)
    block = jax.ShapeDtypeStruct(blocks[0].shape, bf16)
    flops = 4 * 5 * 2 * slots * model * (blocks[0].shape[0] // 2)
    return pl.pallas_call(
        experts_kernel,
        out_shape=(block,) * 4
        + (
            jax.ShapeDtypeStruct((slots, model), bf16),
            jax.ShapeDtypeStruct((slots, LANES), f32),
        ),
        in_specs=[anywhere] * 5,
        out_specs=(anywhere,) * 4 + (vmem, vmem),
        scratch_shapes=[
            pltpu.VMEM(rows.shape, bf16),
            pltpu.VMEM((4,) + blocks[0].shape, bf16),
            pltpu.VMEM((4,) + blocks[0].shape, bf16),
            pltpu.VMEM((slots, model), f32),
            pltpu.SemaphoreType.DMA((5,)),
            pltpu.SemaphoreType.DMA((4,)),
        ],
        cost_estimate=pl.CostEstimate(
            flops=flops, bytes_accessed=2 * (rows.size + 8 * blocks[0].size), transcendentals=0
        ),
        name="experts",
    )(rows, *blocks)


def exchange(x, groups):
    return lax.all_to_all(
        x, AXES, split_axis=0, concat_axis=0, axis_index_groups=groups, tiled=True
    )


def on_device(groups, tokens, d_out, expert_ids, gate_weights, w_in, w_out):
    tok_rows, model = tokens.shape
    width = model // LANES
    experts = len(groups[0])
    slots = 2 * experts
    own = jnp.concatenate([w_in[0].T, w_out[0]], axis=0)
    hidden = own.shape[0] // 2
    oth = lax.ppermute(own, "yl", SWAP)
    outgoing, target = dispatch(
        expert_ids,
        gate_weights,
        tokens.reshape(tok_rows, width, LANES),
        d_out.reshape(tok_rows, width, LANES),
        experts,
    )
    arrived = exchange(outgoing.reshape(experts, 4 * width, LANES), groups)
    oth = hold(oth, HOLD_FLOPS)
    own, oth = lax.optimization_barrier((own, oth))
    blocks = [own, lax.ppermute(own, "core", SWAP), oth, lax.ppermute(oth, "core", SWAP)]
    arrived, *blocks = lax.optimization_barrier((arrived, *blocks))
    rows = arrived.reshape(slots, 2 * model)
    own_grad, peer_grad, far_own, far_peer, dx, gate = run_experts(rows, blocks)
    gate_high = gate.astype(bf16)
    gate_low = (gate - gate_high.astype(f32)).astype(bf16)
    gate_rows = jnp.stack([gate_high, gate_low], axis=1).reshape(experts, 4, LANES)
    gate_rows = jnp.pad(gate_rows, ((0, 0), (0, GATE_ROWS - 4), (0, 0)))
    back = jnp.concatenate([dx.reshape(experts, 2 * width, LANES), gate_rows], axis=1)
    far_peer, back = lax.optimization_barrier((lax.ppermute(far_peer, "core", SWAP), back))
    far = (far_own.astype(f32) + far_peer.astype(f32)).astype(bf16)
    came = hold(lax.ppermute(far, "yl", SWAP), HOLD_FLOPS)
    back, peer_grad, _ = lax.optimization_barrier((back, peer_grad, far))
    near_peer = lax.ppermute(peer_grad, "core", SWAP)
    returned = exchange(back, groups)
    total = own_grad.astype(f32) + near_peer.astype(f32) + came.astype(f32)
    d_first, d_second = total[:hidden].T.astype(bf16), total[hidden:].astype(bf16)
    returned, d_first, d_second = lax.optimization_barrier((returned, d_first, d_second))
    d_tok3, gate_sums = combine(target, returned, tok_rows, width)
    d_gates = gate_sums[:, :TOPK] / gate_weights
    return (d_tok3.reshape(tok_rows, model), d_gates, d_first[None], d_second[None])


def solution(mesh):
    dp, expert = mesh.devices.shape
    pairs = expert // 4
    fine = Mesh(np.asarray(mesh.devices).reshape(dp, pairs, 2, 2), AXES)
    number = np.arange(dp * expert).reshape(dp, pairs, 2, 2)
    near = np.arange(pairs) >= pairs // 2
    groups = [
        [int(number[i, k, int(near[k]) ^ side, c]) for i in range(dp) for k in range(pairs)]
        for side in range(2)
        for c in range(2)
    ]
    flat, block = P(AXES, None), P(AXES, None, None)
    return jax.shard_map(
        functools.partial(on_device, groups),
        mesh=fine,
        in_specs=(flat, flat, flat, flat, block, block),
        out_specs=(flat, flat, block, block),
        check_vma=False,
    )
```

```python
import functools

import jax
import jax.numpy as jnp
import numpy as np
from jax import lax
from jax.experimental import pallas as pl
from jax.experimental.pallas import tpu as pltpu
from jax.sharding import Mesh
from jax.sharding import PartitionSpec as P

TOPK = 4
LANES = 128
AXES = ("dp", "yh", "yl", "core")
GATE_ROWS = 8
HOLD_FLOPS = int(3e10)
SWAP = [(0, 1), (1, 0)]
f32, bf16 = jnp.float32, jnp.bfloat16


def dispatch_kernel(ids_ref, gates_ref, tok_ref, dout_ref, out_ref, target_ref, count_ref):
    tokens, width = tok_ref.shape[0], tok_ref.shape[1]
    out_ref[...] = jnp.zeros_like(out_ref)

    def clear(i, carry):
        count_ref[i] = 0
        return carry

    lax.fori_loop(0, count_ref.shape[0], clear, 0, unroll=8)

    def place(t, carry):
        row = tok_ref[t]
        grad = dout_ref[t].astype(f32)
        for k in range(TOPK):
            e = ids_ref[t, k]
            slot = count_ref[e]
            count_ref[e] = slot + 1
            at = 2 * e + slot
            target_ref[t, k] = at
            out_ref[at, 0:width, :] = row
            out_ref[at, width : 2 * width, :] = (grad * gates_ref[t, k]).astype(bf16)
        return carry

    lax.fori_loop(0, tokens, place, 0)


def dispatch(ids, gates, tok3, dout3, experts):
    tokens, width, _ = tok3.shape
    smem = pl.BlockSpec(memory_space=pltpu.SMEM)
    vmem = pl.BlockSpec(memory_space=pltpu.VMEM)
    return pl.pallas_call(
        dispatch_kernel,
        out_shape=(
            jax.ShapeDtypeStruct((2 * experts, 2 * width, LANES), bf16),
            jax.ShapeDtypeStruct((tokens, TOPK), jnp.int32),
        ),
        in_specs=[smem, smem, vmem, vmem],
        out_specs=(vmem, smem),
        scratch_shapes=[pltpu.SMEM((experts,), jnp.int32)],
        name="dispatch",
    )(ids, gates, tok3, dout3)


def hold(x, flops):
    anywhere = pl.BlockSpec(memory_space=pl.ANY)
    return pl.pallas_call(
        lambda x_ref, y_ref: None,
        out_shape=jax.ShapeDtypeStruct(x.shape, x.dtype),
        in_specs=[anywhere],
        out_specs=anywhere,
        input_output_aliases={0: 0},
        cost_estimate=pl.CostEstimate(flops=flops, bytes_accessed=0, transcendentals=0),
        name="hold",
    )(x)


def combine_kernel(target_ref, back_ref, gates_ref, dx_ref, gate_ref, dx_rows, gate_rows):
    tokens, model = dx_ref.shape
    width = model // LANES
    lane = lax.broadcasted_iota(jnp.int32, (1, LANES), 1)

    def total(t, carry):
        acc = jnp.zeros((width, LANES), f32)
        gate = jnp.zeros((1, LANES), f32)
        for k in range(TOPK):
            at = target_ref[t, k]
            e, slot = lax.shift_right_logical(at, 1), lax.bitwise_and(at, 1)
            first = pl.multiple_of(slot * width, width)
            acc += back_ref[e, pl.ds(first, width), :].astype(f32)
            extra = back_ref[e, 2 * width : 2 * width + GATE_ROWS, :].astype(f32)
            pair = jnp.where(slot == 0, extra[0:2, :], extra[2:4, :])
            gate = jnp.where(lane == k, pair[0:1, :] + pair[1:2, :], gate)
        dx_rows[pl.ds(pl.multiple_of(t * width, width), width), :] = acc
        gate_rows[pl.ds(t, 1), :] = gate
        return carry

    lax.fori_loop(0, tokens, total, 0)
    for j in range(width):
        part = dx_rows[pl.ds(j, tokens, stride=width), :]
        dx_ref[:, j * LANES : (j + 1) * LANES] = part.astype(bf16)
    gate_ref[...] = gate_rows[:, :TOPK] / gates_ref[...]


def combine(target, back, gates, model):
    tokens = gates.shape[0]
    vmem = pl.BlockSpec(memory_space=pltpu.VMEM)
    return pl.pallas_call(
        combine_kernel,
        out_shape=(
            jax.ShapeDtypeStruct((tokens, model), bf16),
            jax.ShapeDtypeStruct(gates.shape, f32),
        ),
        in_specs=[pl.BlockSpec(memory_space=pltpu.SMEM), vmem, vmem],
        out_specs=(vmem, vmem),
        scratch_shapes=[
            pltpu.VMEM((tokens * model // LANES, LANES), f32),
            pltpu.VMEM((tokens, LANES), f32),
        ],
        name="combine",
    )(target, back, gates)


def dot(a, b, ca, cb):
    return lax.dot_general(a, b, (((ca,), (cb,)), ((), ())), preferred_element_type=f32)


def expert_half(rows_hbm, blocks, stores_to, rows, ins, outs, grads, total, in_sems, out_sems):
    hidden, model = outs.shape[1], outs.shape[2]
    loads = [pltpu.make_async_copy(rows_hbm, rows, in_sems.at[0])]
    for q in range(2):
        loads.append(pltpu.make_async_copy(blocks[2 * q], ins.at[q], in_sems.at[1 + 2 * q]))
        loads.append(pltpu.make_async_copy(blocks[2 * q + 1], outs.at[q], in_sems.at[2 + 2 * q]))
    stores = [
        pltpu.make_async_copy(grads.at[q], g, out_sems.at[q]) for q, g in enumerate(stores_to)
    ]
    for load in loads:
        load.start()
    loads[0].wait()
    gate = jnp.zeros((rows.shape[0], 1), f32)
    for q in range(2):
        loads[1 + 2 * q].wait()
        loads[2 + 2 * q].wait()
        preact = dot(rows[:, :model], ins[q], 1, 0)
        pulled = dot(rows[:, model:], outs[q], 1, 1)
        sig = jax.nn.sigmoid(preact)
        act = preact * sig
        d_pre = (pulled * sig * (1.0 + preact * (1.0 - sig))).astype(bf16)
        gate += jnp.sum(act * pulled, axis=1, keepdims=True)
        act = act.astype(bf16)
        grads[q, :hidden, :] = dot(d_pre, rows[:, :model], 0, 0).astype(bf16)
        grads[q, hidden:, :] = dot(act, rows[:, model:], 0, 0).astype(bf16)
        stores[q].start()
        total[...] += dot(d_pre, ins[q], 1, 1)
    return gate, stores


def far_kernel(rows_hbm, i0, o0, i1, o1, g0, g1, dx_ref, gate_ref, *scratch):
    dx_ref[...] = jnp.zeros_like(dx_ref)
    rows, ins, outs, grads, in_sems, out_sems = scratch
    gate, stores = expert_half(
        rows_hbm, (i0, o0, i1, o1), (g0, g1), rows, ins, outs, grads, dx_ref, in_sems, out_sems
    )
    gate_ref[...] = jnp.broadcast_to(gate, gate_ref.shape)
    for store in stores:
        store.wait()


def near_kernel(
    rows_hbm, i0, o0, i1, o1, dx_in, gate_in, g0, g1, back_ref, rows, ins, outs, grads, total, lines, in_sems, out_sems
):
    slots, model = total.shape
    width = model // LANES
    total[...] = dx_in[...]
    gate, stores = expert_half(
        rows_hbm, (i0, o0, i1, o1), (g0, g1), rows, ins, outs, grads, total, in_sems, out_sems
    )
    for j in range(width):
        lines[pl.ds(j, slots, stride=width), :] = total[:, j * LANES : (j + 1) * LANES]
    experts = slots // 2
    back_ref[:, : 2 * width, :] = lines[...].astype(bf16).reshape(experts, 2 * width, LANES)
    gate = gate_in[...] + gate
    high = gate.astype(bf16)
    low = (gate - high.astype(f32)).astype(bf16)
    row = lax.broadcasted_iota(jnp.int32, (experts * GATE_ROWS, slots), 0)
    slot = lax.broadcasted_iota(jnp.int32, (experts * GATE_ROWS, slots), 1)
    place = row - (slot >> 1) * GATE_ROWS - 2 * (slot & 1)
    spread = dot((place == 0).astype(bf16), high, 1, 0) + dot((place == 1).astype(bf16), low, 1, 0)
    back_ref[:, 2 * width :, :] = spread.astype(bf16).reshape(experts, GATE_ROWS, LANES)
    for store in stores:
        store.wait()


def run_experts(rows, blocks, carried=None):
    slots, model = rows.shape[0], rows.shape[1] // 2
    hidden = blocks[1].shape[0]
    width = model // LANES
    anywhere = pl.BlockSpec(memory_space=pl.ANY)
    vmem = pl.BlockSpec(memory_space=pltpu.VMEM)
    grad = jax.ShapeDtypeStruct((2 * hidden, model), bf16)
    scratch = [
        pltpu.VMEM(rows.shape, bf16),
        pltpu.VMEM((2, model, hidden), bf16),
        pltpu.VMEM((2, hidden, model), bf16),
        pltpu.VMEM((2, 2 * hidden, model), bf16),
    ]
    sems = [pltpu.SemaphoreType.DMA((5,)), pltpu.SemaphoreType.DMA((2,))]
    cost = pl.CostEstimate(
        flops=2 * 5 * 2 * slots * model * hidden,
        bytes_accessed=2 * (rows.size + 12 * hidden * model),
        transcendentals=0,
    )
    if carried is None:
        return pl.pallas_call(
            far_kernel,
            out_shape=(
                grad,
                grad,
                jax.ShapeDtypeStruct((slots, model), f32),
                jax.ShapeDtypeStruct((slots, LANES), f32),
            ),
            in_specs=[anywhere] * 5,
            out_specs=(anywhere, anywhere, vmem, vmem),
            scratch_shapes=scratch + sems,
            cost_estimate=cost,
            name="far_quarters",
        )(rows, *blocks)
    return pl.pallas_call(
        near_kernel,
        out_shape=(
            grad,
            grad,
            jax.ShapeDtypeStruct((slots // 2, 2 * width + GATE_ROWS, LANES), bf16),
        ),
        in_specs=[anywhere] * 5 + [vmem, vmem],
        out_specs=(anywhere, anywhere, vmem),
        scratch_shapes=scratch
        + [pltpu.VMEM((slots, model), f32), pltpu.VMEM((slots * width, LANES), f32)]
        + sems,
        cost_estimate=cost,
        name="near_quarters",
    )(rows, *blocks, *carried)


def finish_kernel(own_ref, peer_ref, came_ref, first_ref, second_ref):
    hidden = second_ref.shape[0]
    total = own_ref[...].astype(f32) + peer_ref[...].astype(f32) + came_ref[...].astype(f32)
    first_ref[...] = total[:hidden, :].T.astype(bf16)
    second_ref[...] = total[hidden:, :].astype(bf16)


def finish(own, peer, came):
    hidden, model = own.shape[0] // 2, own.shape[1]
    part = pl.BlockSpec((2 * hidden, 512), lambda j: (0, j))
    return pl.pallas_call(
        finish_kernel,
        grid=(model // 512,),
        out_shape=(
            jax.ShapeDtypeStruct((model, hidden), bf16),
            jax.ShapeDtypeStruct((hidden, model), bf16),
        ),
        in_specs=[part] * 3,
        out_specs=(
            pl.BlockSpec((512, hidden), lambda j: (j, 0)),
            pl.BlockSpec((hidden, 512), lambda j: (0, j)),
        ),
        name="finish",
    )(own, peer, came)


def exchange(x, groups):
    return lax.all_to_all(
        x, AXES, split_axis=0, concat_axis=0, axis_index_groups=groups, tiled=True
    )


def on_device(groups, tokens, d_out, expert_ids, gate_weights, w_in, w_out):
    tok_rows, model = tokens.shape
    width = model // LANES
    experts = len(groups[0])
    slots = 2 * experts
    own_in, own_out = w_in[0], w_out[0]
    oth_in = lax.ppermute(own_in, "yl", SWAP)
    oth_out = lax.ppermute(own_out, "yl", SWAP)
    outgoing, target = dispatch(
        expert_ids,
        gate_weights,
        tokens.reshape(tok_rows, width, LANES),
        d_out.reshape(tok_rows, width, LANES),
        experts,
    )
    arrived = exchange(outgoing.reshape(experts, 4 * width, LANES), groups)
    own_in, own_out, oth_in = lax.optimization_barrier((own_in, own_out, hold(oth_in, HOLD_FLOPS)))
    oth_out = hold(oth_out, HOLD_FLOPS)
    near = [own_in, own_out, lax.ppermute(own_in, "core", SWAP), lax.ppermute(own_out, "core", SWAP)]
    far = [oth_in, oth_out, lax.ppermute(oth_in, "core", SWAP), lax.ppermute(oth_out, "core", SWAP)]
    arrived, *blocks = lax.optimization_barrier((arrived, *near, *far))
    rows = arrived.reshape(slots, 2 * model)
    far_own, far_peer, dx, gate = run_experts(rows, blocks[4:])
    own_grad, peer_grad, back = run_experts(rows, blocks[:4], (dx, gate))
    far_peer, back = lax.optimization_barrier((lax.ppermute(far_peer, "core", SWAP), back))
    far_sum = (far_own.astype(f32) + far_peer.astype(f32)).astype(bf16)
    came = hold(lax.ppermute(far_sum, "yl", SWAP), HOLD_FLOPS)
    back, peer_grad, _ = lax.optimization_barrier((back, peer_grad, far_sum))
    near_peer = lax.ppermute(peer_grad, "core", SWAP)
    returned = exchange(back, groups)
    d_first, d_second = finish(own_grad, near_peer, came)
    returned, d_first, d_second = lax.optimization_barrier((returned, d_first, d_second))
    d_tokens, d_gates = combine(target, returned, gate_weights, model)
    return (d_tokens, d_gates, d_first[None], d_second[None])


def solution(mesh):
    dp, expert = mesh.devices.shape
    pairs = expert // 4
    fine = Mesh(np.asarray(mesh.devices).reshape(dp, pairs, 2, 2), AXES)
    number = np.arange(dp * expert).reshape(dp, pairs, 2, 2)
    near = np.arange(pairs) >= pairs // 2
    groups = [
        [int(number[i, k, int(near[k]) ^ side, c]) for i in range(dp) for k in range(pairs)]
        for side in range(2)
        for c in range(2)
    ]
    flat, block = P(AXES, None), P(AXES, None, None)
    return jax.shard_map(
        functools.partial(on_device, groups),
        mesh=fine,
        in_specs=(flat, flat, flat, flat, block, block),
        out_specs=(flat, flat, block, block),
        check_vma=False,
    )
```

```python
import functools

import jax
import jax.numpy as jnp
import numpy as np
from jax import lax
from jax.experimental import pallas as pl
from jax.experimental.pallas import tpu as pltpu
from jax.sharding import Mesh
from jax.sharding import PartitionSpec as P

TOPK = 4
LANES = 128
AXES = ("dp", "yh", "yl", "core")
GATE_ROWS = 8
HOLD_FLOPS = int(3e10)
SWAP = [(0, 1), (1, 0)]
f32, bf16 = jnp.float32, jnp.bfloat16


def dispatch_kernel(
    ids_ref, gates_ref, tok_ref, dout_ref, out_ref, target_ref, count_ref, tok_lines, dout_lines
):
    tokens, model = tok_ref.shape
    width = model // LANES
    for j in range(width):
        part = slice(j * LANES, (j + 1) * LANES)
        tok_lines[pl.ds(j, tokens, stride=width), :] = tok_ref[:, part].astype(f32)
        dout_lines[pl.ds(j, tokens, stride=width), :] = dout_ref[:, part].astype(f32)
    out_ref[...] = jnp.zeros_like(out_ref)

    def clear(i, carry):
        count_ref[i] = 0
        return carry

    lax.fori_loop(0, count_ref.shape[0], clear, 0, unroll=8)

    def place(t, carry):
        lines = pl.ds(pl.multiple_of(t * width, width), width)
        row = tok_lines[lines, :].astype(bf16)
        grad = dout_lines[lines, :]
        for k in range(TOPK):
            e = ids_ref[k, t]
            slot = count_ref[e]
            count_ref[e] = slot + 1
            at = 2 * e + slot
            target_ref[k, t] = at
            out_ref[at, 0:width, :] = row
            out_ref[at, width : 2 * width, :] = (grad * gates_ref[k, t]).astype(bf16)
        return carry

    lax.fori_loop(0, tokens, place, 0)


def dispatch(ids, gates, tokens, d_out, experts):
    rows, model = tokens.shape
    width = model // LANES
    smem = pl.BlockSpec(memory_space=pltpu.SMEM)
    vmem = pl.BlockSpec(memory_space=pltpu.VMEM)
    return pl.pallas_call(
        dispatch_kernel,
        out_shape=(
            jax.ShapeDtypeStruct((2 * experts, 2 * width, LANES), bf16),
            jax.ShapeDtypeStruct((TOPK, rows), jnp.int32),
        ),
        in_specs=[smem, smem, vmem, vmem],
        out_specs=(vmem, smem),
        scratch_shapes=[
            pltpu.SMEM((experts,), jnp.int32),
            pltpu.VMEM((rows * width, LANES), f32),
            pltpu.VMEM((rows * width, LANES), f32),
        ],
        name="dispatch",
    )(ids, gates, tokens, d_out)


def hold(x, flops):
    anywhere = pl.BlockSpec(memory_space=pl.ANY)
    return pl.pallas_call(
        lambda x_ref, y_ref: None,
        out_shape=jax.ShapeDtypeStruct(x.shape, x.dtype),
        in_specs=[anywhere],
        out_specs=anywhere,
        input_output_aliases={0: 0},
        cost_estimate=pl.CostEstimate(flops=flops, bytes_accessed=0, transcendentals=0),
        name="hold",
    )(x)


def combine_kernel(target_ref, back_ref, gates_ref, dx_ref, gate_ref, dx_rows, gate_rows):
    tokens, model = dx_ref.shape
    width = model // LANES
    lane = lax.broadcasted_iota(jnp.int32, (1, LANES), 1)

    def total(t, carry):
        acc = jnp.zeros((width, LANES), f32)
        gate = jnp.zeros((1, LANES), f32)
        for k in range(TOPK):
            at = target_ref[k, t]
            e, slot = lax.shift_right_logical(at, 1), lax.bitwise_and(at, 1)
            first = pl.multiple_of(slot * width, width)
            acc += back_ref[e, pl.ds(first, width), :].astype(f32)
            extra = back_ref[e, 2 * width : 2 * width + GATE_ROWS, :].astype(f32)
            pair = jnp.where(slot == 0, extra[0:2, :], extra[2:4, :])
            gate = jnp.where(lane == k, pair[0:1, :] + pair[1:2, :], gate)
        dx_rows[pl.ds(pl.multiple_of(t * width, width), width), :] = acc
        gate_rows[pl.ds(t, 1), :] = gate
        return carry

    lax.fori_loop(0, tokens, total, 0)
    for j in range(width):
        part = dx_rows[pl.ds(j, tokens, stride=width), :]
        dx_ref[:, j * LANES : (j + 1) * LANES] = part.astype(bf16)
    gate_ref[...] = gate_rows[...].T[:TOPK, :] / gates_ref[...]


def combine(target, back, gates, model):
    tokens = gates.shape[1]
    vmem = pl.BlockSpec(memory_space=pltpu.VMEM)
    return pl.pallas_call(
        combine_kernel,
        out_shape=(
            jax.ShapeDtypeStruct((tokens, model), bf16),
            jax.ShapeDtypeStruct(gates.shape, f32),
        ),
        in_specs=[pl.BlockSpec(memory_space=pltpu.SMEM), vmem, vmem],
        out_specs=(vmem, vmem),
        scratch_shapes=[
            pltpu.VMEM((tokens * model // LANES, LANES), f32),
            pltpu.VMEM((tokens, LANES), f32),
        ],
        name="combine",
    )(target, back, gates)


def dot(a, b, ca, cb):
    return lax.dot_general(a, b, (((ca,), (cb,)), ((), ())), preferred_element_type=f32)


def experts_kernel(rows_hbm, *refs):
    blocks, stores_to, back_ref = refs[:8], refs[8:12], refs[12]
    rows, ins, outs, grads, total, lines, in_sems, out_sems = refs[13:]
    hidden, model = outs.shape[1], outs.shape[2]
    slots, width = rows.shape[0], model // LANES
    experts = slots // 2
    loads = [pltpu.make_async_copy(rows_hbm, rows, in_sems.at[0])]
    for q in range(4):
        loads.append(pltpu.make_async_copy(blocks[2 * q], ins.at[q], in_sems.at[1 + 2 * q]))
        loads.append(pltpu.make_async_copy(blocks[2 * q + 1], outs.at[q], in_sems.at[2 + 2 * q]))
    stores = [
        pltpu.make_async_copy(grads.at[q], g, out_sems.at[q]) for q, g in enumerate(stores_to)
    ]
    for load in loads:
        load.start()
    loads[0].wait()
    gate = jnp.zeros((slots, 1), f32)
    for q in range(4):
        loads[1 + 2 * q].wait()
        loads[2 + 2 * q].wait()
        preact = dot(rows[:, :model], ins[q], 1, 0)
        pulled = dot(rows[:, model:], outs[q], 1, 1)
        sig = jax.nn.sigmoid(preact)
        act = preact * sig
        d_pre = (pulled * sig * (1.0 + preact * (1.0 - sig))).astype(bf16)
        gate += jnp.sum(act * pulled, axis=1, keepdims=True)
        act = act.astype(bf16)
        grads[q, :hidden, :] = dot(d_pre, rows[:, :model], 0, 0).astype(bf16)
        grads[q, hidden:, :] = dot(act, rows[:, model:], 0, 0).astype(bf16)
        stores[q].start()
        part = dot(d_pre, ins[q], 1, 1)
        total[...] = part if q == 0 else total[...] + part
    for j in range(width):
        lines[pl.ds(j, slots, stride=width), :] = total[:, j * LANES : (j + 1) * LANES]
    back_ref[:, : 2 * width, :] = lines[...].astype(bf16).reshape(experts, 2 * width, LANES)
    gate = jnp.broadcast_to(gate, (slots, LANES))
    high = gate.astype(bf16)
    low = (gate - high.astype(f32)).astype(bf16)
    row = lax.broadcasted_iota(jnp.int32, (experts * GATE_ROWS, slots), 0)
    slot = lax.broadcasted_iota(jnp.int32, (experts * GATE_ROWS, slots), 1)
    place = row - (slot >> 1) * GATE_ROWS - 2 * (slot & 1)
    spread = dot((place == 0).astype(bf16), high, 1, 0) + dot((place == 1).astype(bf16), low, 1, 0)
    back_ref[:, 2 * width :, :] = spread.astype(bf16).reshape(experts, GATE_ROWS, LANES)
    for store in stores:
        store.wait()


def run_experts(rows, blocks):
    slots, model = rows.shape[0], rows.shape[1] // 2
    hidden = blocks[1].shape[0]
    width = model // LANES
    anywhere = pl.BlockSpec(memory_space=pl.ANY)
    vmem = pl.BlockSpec(memory_space=pltpu.VMEM)
    return pl.pallas_call(
        experts_kernel,
        out_shape=(jax.ShapeDtypeStruct((2 * hidden, model), bf16),) * 4
        + (jax.ShapeDtypeStruct((slots // 2, 2 * width + GATE_ROWS, LANES), bf16),),
        in_specs=[anywhere] * 9,
        out_specs=(anywhere,) * 4 + (vmem,),
        scratch_shapes=[
            pltpu.VMEM(rows.shape, bf16),
            pltpu.VMEM((4, model, hidden), bf16),
            pltpu.VMEM((4, hidden, model), bf16),
            pltpu.VMEM((4, 2 * hidden, model), bf16),
            pltpu.VMEM((slots, model), f32),
            pltpu.VMEM((slots * width, LANES), f32),
            pltpu.SemaphoreType.DMA((9,)),
            pltpu.SemaphoreType.DMA((4,)),
        ],
        cost_estimate=pl.CostEstimate(
            flops=4 * 5 * 2 * slots * model * hidden,
            bytes_accessed=2 * (rows.size + 16 * hidden * model),
            transcendentals=0,
        ),
        name="experts",
    )(rows, *blocks)


def finish_kernel(own_ref, peer_ref, came_ref, first_ref, second_ref):
    hidden = second_ref.shape[0]
    total = own_ref[...].astype(f32) + peer_ref[...].astype(f32) + came_ref[...].astype(f32)
    first_ref[...] = total[:hidden, :].T.astype(bf16)
    second_ref[...] = total[hidden:, :].astype(bf16)


def finish(own, peer, came):
    hidden, model = own.shape[0] // 2, own.shape[1]
    part = pl.BlockSpec((2 * hidden, 512), lambda j: (0, j))
    return pl.pallas_call(
        finish_kernel,
        grid=(model // 512,),
        out_shape=(
            jax.ShapeDtypeStruct((model, hidden), bf16),
            jax.ShapeDtypeStruct((hidden, model), bf16),
        ),
        in_specs=[part] * 3,
        out_specs=(
            pl.BlockSpec((512, hidden), lambda j: (j, 0)),
            pl.BlockSpec((hidden, 512), lambda j: (0, j)),
        ),
        name="finish",
    )(own, peer, came)


def exchange(x, groups):
    return lax.all_to_all(
        x, AXES, split_axis=0, concat_axis=0, axis_index_groups=groups, tiled=True
    )


def on_device(groups, tokens, d_out, expert_ids, gate_weights, w_in, w_out):
    tok_rows, model = tokens.shape
    width = model // LANES
    experts = len(groups[0])
    slots = 2 * experts
    own_in, own_out = w_in[0], w_out[0]
    gates = gate_weights.T
    oth_in = hold(lax.ppermute(own_in, "yl", SWAP), HOLD_FLOPS)
    outgoing, target = dispatch(expert_ids.T, gates, tokens, d_out, experts)
    arrived = exchange(outgoing.reshape(experts, 4 * width, LANES), groups)
    own_in, own_out, oth_in = lax.optimization_barrier((own_in, own_out, oth_in))
    oth_out = lax.ppermute(own_out, "yl", SWAP)
    near = [own_in, own_out, lax.ppermute(own_in, "core", SWAP), lax.ppermute(own_out, "core", SWAP)]
    far = [oth_in, oth_out, lax.ppermute(oth_in, "core", SWAP), lax.ppermute(oth_out, "core", SWAP)]
    arrived, *blocks = lax.optimization_barrier((arrived, *near, *far))
    rows = arrived.reshape(slots, 2 * model)
    own_grad, peer_grad, far_own, far_peer, back = run_experts(rows, blocks)
    returned = exchange(back, groups)
    far_peer = hold(lax.ppermute(far_peer, "core", SWAP), HOLD_FLOPS)
    far_sum = (far_own.astype(f32) + far_peer.astype(f32)).astype(bf16)
    came = lax.ppermute(far_sum, "yl", SWAP)
    near_peer = lax.ppermute(peer_grad, "core", SWAP)
    d_tokens, d_gates = combine(target, returned, gates, model)
    came, d_tokens, d_gates = lax.optimization_barrier((came, d_tokens, d_gates))
    d_first, d_second = finish(own_grad, near_peer, came)
    return (d_tokens, d_gates.T, d_first[None], d_second[None])


def solution(mesh):
    dp, expert = mesh.devices.shape
    pairs = expert // 4
    fine = Mesh(np.asarray(mesh.devices).reshape(dp, pairs, 2, 2), AXES)
    number = np.arange(dp * expert).reshape(dp, pairs, 2, 2)
    near = np.arange(pairs) >= pairs // 2
    groups = [
        [int(number[i, k, int(near[k]) ^ side, c]) for i in range(dp) for k in range(pairs)]
        for side in range(2)
        for c in range(2)
    ]
    flat, block = P(AXES, None), P(AXES, None, None)
    return jax.shard_map(
        functools.partial(on_device, groups),
        mesh=fine,
        in_specs=(flat, flat, flat, flat, block, block),
        out_specs=(flat, flat, block, block),
        check_vma=False,
    )
```

```python
import functools

import jax
import jax.numpy as jnp
import numpy as np
from jax import lax
from jax.experimental import pallas as pl
from jax.experimental.pallas import tpu as pltpu
from jax.sharding import Mesh
from jax.sharding import PartitionSpec as P

TOPK = 4
LANES = 128
AXES = ("dp", "yh", "yl", "core")
GATE_ROWS = 8
HOLD_FLOPS = int(3e10)
SWAP = [(0, 1), (1, 0)]
f32, bf16 = jnp.float32, jnp.bfloat16


def dispatch_kernel(
    ids_ref, gates_ref, tok_ref, dout_ref, out_ref, target_ref, count_ref, tok_lines, dout_lines
):
    tokens, model = tok_ref.shape
    width = model // LANES
    for j in range(width):
        part = slice(j * LANES, (j + 1) * LANES)
        tok_lines[pl.ds(j, tokens, stride=width), :] = tok_ref[:, part].astype(f32)
        dout_lines[pl.ds(j, tokens, stride=width), :] = dout_ref[:, part].astype(f32)
    out_ref[...] = jnp.zeros_like(out_ref)

    def clear(i, carry):
        count_ref[i] = 0
        return carry

    lax.fori_loop(0, count_ref.shape[0], clear, 0, unroll=8)

    def place(t, carry):
        lines = pl.ds(pl.multiple_of(t * width, width), width)
        row = tok_lines[lines, :].astype(bf16)
        grad = dout_lines[lines, :]
        for k in range(TOPK):
            e = ids_ref[k, t]
            slot = count_ref[e]
            count_ref[e] = slot + 1
            at = 2 * e + slot
            target_ref[k, t] = at
            out_ref[at, 0:width, :] = row
            out_ref[at, width : 2 * width, :] = (grad * gates_ref[k, t]).astype(bf16)
        return carry

    lax.fori_loop(0, tokens, place, 0)


def dispatch(ids, gates, tokens, d_out, experts):
    rows, model = tokens.shape
    width = model // LANES
    smem = pl.BlockSpec(memory_space=pltpu.SMEM)
    vmem = pl.BlockSpec(memory_space=pltpu.VMEM)
    return pl.pallas_call(
        dispatch_kernel,
        out_shape=(
            jax.ShapeDtypeStruct((2 * experts, 2 * width, LANES), bf16),
            jax.ShapeDtypeStruct((TOPK, rows), jnp.int32),
        ),
        in_specs=[smem, smem, vmem, vmem],
        out_specs=(vmem, smem),
        scratch_shapes=[
            pltpu.SMEM((experts,), jnp.int32),
            pltpu.VMEM((rows * width, LANES), f32),
            pltpu.VMEM((rows * width, LANES), f32),
        ],
        name="dispatch",
    )(ids, gates, tokens, d_out)


def hold(x, flops):
    anywhere = pl.BlockSpec(memory_space=pl.ANY)
    return pl.pallas_call(
        lambda x_ref, y_ref: None,
        out_shape=jax.ShapeDtypeStruct(x.shape, x.dtype),
        in_specs=[anywhere],
        out_specs=anywhere,
        input_output_aliases={0: 0},
        cost_estimate=pl.CostEstimate(flops=flops, bytes_accessed=0, transcendentals=0),
        name="hold",
    )(x)


def combine_kernel(target_ref, back_ref, gates_ref, dx_ref, gate_ref, dx_rows, gate_rows):
    tokens, model = dx_ref.shape
    width = model // LANES
    lane = lax.broadcasted_iota(jnp.int32, (1, LANES), 1)

    def total(t, carry):
        acc = jnp.zeros((width, LANES), f32)
        gate = jnp.zeros((1, LANES), f32)
        for k in range(TOPK):
            at = target_ref[k, t]
            e, slot = lax.shift_right_logical(at, 1), lax.bitwise_and(at, 1)
            first = pl.multiple_of(slot * width, width)
            acc += back_ref[e, pl.ds(first, width), :].astype(f32)
            extra = back_ref[e, 2 * width : 2 * width + GATE_ROWS, :].astype(f32)
            pair = jnp.where(slot == 0, extra[0:2, :], extra[2:4, :])
            gate = jnp.where(lane == k, pair[0:1, :] + pair[1:2, :], gate)
        dx_rows[pl.ds(pl.multiple_of(t * width, width), width), :] = acc
        gate_rows[pl.ds(t, 1), :] = gate
        return carry

    lax.fori_loop(0, tokens, total, 0)
    for j in range(width):
        part = dx_rows[pl.ds(j, tokens, stride=width), :]
        dx_ref[:, j * LANES : (j + 1) * LANES] = part.astype(bf16)
    gate_ref[...] = gate_rows[...].T[:TOPK, :] / gates_ref[...]


def combine(target, back, gates, model):
    tokens = gates.shape[1]
    vmem = pl.BlockSpec(memory_space=pltpu.VMEM)
    return pl.pallas_call(
        combine_kernel,
        out_shape=(
            jax.ShapeDtypeStruct((tokens, model), bf16),
            jax.ShapeDtypeStruct(gates.shape, f32),
        ),
        in_specs=[pl.BlockSpec(memory_space=pltpu.SMEM), vmem, vmem],
        out_specs=(vmem, vmem),
        scratch_shapes=[
            pltpu.VMEM((tokens * model // LANES, LANES), f32),
            pltpu.VMEM((tokens, LANES), f32),
        ],
        name="combine",
    )(target, back, gates)


def dot(a, b, ca, cb):
    return lax.dot_general(a, b, (((ca,), (cb,)), ((), ())), preferred_element_type=f32)


def experts_kernel(rows_hbm, *refs):
    blocks, stores_to, back_ref = refs[:8], refs[8:16], refs[16]
    rows, ins, outs, grads, total, lines, in_sems, out_sems = refs[17:]
    hidden, model = outs.shape[1], outs.shape[2]
    slots, width = rows.shape[0], model // LANES
    experts = slots // 2
    loads = [pltpu.make_async_copy(rows_hbm, rows, in_sems.at[0])]
    for q in range(4):
        loads.append(pltpu.make_async_copy(blocks[2 * q], ins.at[q], in_sems.at[1 + 2 * q]))
        loads.append(pltpu.make_async_copy(blocks[2 * q + 1], outs.at[q], in_sems.at[2 + 2 * q]))
    stores = [
        pltpu.make_async_copy(grads.at[q], g, out_sems.at[q]) for q, g in enumerate(stores_to)
    ]
    for load in loads:
        load.start()
    loads[0].wait()
    gate = jnp.zeros((slots, 1), f32)
    for q in range(4):
        loads[1 + 2 * q].wait()
        loads[2 + 2 * q].wait()
        preact = dot(rows[:, :model], ins[q], 1, 0)
        pulled = dot(rows[:, model:], outs[q], 1, 1)
        sig = jax.nn.sigmoid(preact)
        act = preact * sig
        d_pre = (pulled * sig * (1.0 + preact * (1.0 - sig))).astype(bf16)
        gate += jnp.sum(act * pulled, axis=1, keepdims=True)
        act = act.astype(bf16)
        grads[2 * q] = dot(d_pre, rows[:, :model], 0, 0).astype(bf16)
        grads[2 * q + 1] = dot(act, rows[:, model:], 0, 0).astype(bf16)
        stores[2 * q].start()
        stores[2 * q + 1].start()
        part = dot(d_pre, ins[q], 1, 1)
        total[...] = part if q == 0 else total[...] + part
    for j in range(width):
        lines[pl.ds(j, slots, stride=width), :] = total[:, j * LANES : (j + 1) * LANES]
    back_ref[:, : 2 * width, :] = lines[...].astype(bf16).reshape(experts, 2 * width, LANES)
    gate = jnp.broadcast_to(gate, (slots, LANES))
    high = gate.astype(bf16)
    low = (gate - high.astype(f32)).astype(bf16)
    row = lax.broadcasted_iota(jnp.int32, (experts * GATE_ROWS, slots), 0)
    slot = lax.broadcasted_iota(jnp.int32, (experts * GATE_ROWS, slots), 1)
    place = row - (slot >> 1) * GATE_ROWS - 2 * (slot & 1)
    spread = dot((place == 0).astype(bf16), high, 1, 0) + dot((place == 1).astype(bf16), low, 1, 0)
    back_ref[:, 2 * width :, :] = spread.astype(bf16).reshape(experts, GATE_ROWS, LANES)
    for store in stores:
        store.wait()


def run_experts(rows, blocks):
    slots, model = rows.shape[0], rows.shape[1] // 2
    hidden = blocks[1].shape[0]
    width = model // LANES
    anywhere = pl.BlockSpec(memory_space=pl.ANY)
    vmem = pl.BlockSpec(memory_space=pltpu.VMEM)
    return pl.pallas_call(
        experts_kernel,
        out_shape=(jax.ShapeDtypeStruct((hidden, model), bf16),) * 8
        + (jax.ShapeDtypeStruct((slots // 2, 2 * width + GATE_ROWS, LANES), bf16),),
        in_specs=[anywhere] * 9,
        out_specs=(anywhere,) * 8 + (vmem,),
        scratch_shapes=[
            pltpu.VMEM(rows.shape, bf16),
            pltpu.VMEM((4, model, hidden), bf16),
            pltpu.VMEM((4, hidden, model), bf16),
            pltpu.VMEM((8, hidden, model), bf16),
            pltpu.VMEM((slots, model), f32),
            pltpu.VMEM((slots * width, LANES), f32),
            pltpu.SemaphoreType.DMA((9,)),
            pltpu.SemaphoreType.DMA((8,)),
        ],
        cost_estimate=pl.CostEstimate(
            flops=4 * 5 * 2 * slots * model * hidden,
            bytes_accessed=2 * (rows.size + 16 * hidden * model),
            transcendentals=0,
        ),
        name="experts",
    )(rows, *blocks)


def finish_kernel(flip, own_ref, peer_ref, came_ref, out_ref):
    total = own_ref[...].astype(f32) + peer_ref[...].astype(f32) + came_ref[...].astype(f32)
    out_ref[...] = (total.T if flip else total).astype(bf16)


def finish(own, peer, came, flip):
    hidden, model = own.shape
    part = pl.BlockSpec((hidden, 512), lambda j: (0, j))
    return pl.pallas_call(
        functools.partial(finish_kernel, flip),
        grid=(model // 512,),
        out_shape=jax.ShapeDtypeStruct((model, hidden) if flip else (hidden, model), bf16),
        in_specs=[part] * 3,
        out_specs=pl.BlockSpec((512, hidden), lambda j: (j, 0)) if flip else part,
        cost_estimate=pl.CostEstimate(flops=0, bytes_accessed=8 * own.size, transcendentals=0),
        name="finish",
    )(own, peer, came)


def exchange(x, groups):
    return lax.all_to_all(
        x, AXES, split_axis=0, concat_axis=0, axis_index_groups=groups, tiled=True
    )


def on_device(groups, tokens, d_out, expert_ids, gate_weights, w_in, w_out):
    tok_rows, model = tokens.shape
    width = model // LANES
    experts = len(groups[0])
    slots = 2 * experts
    own_in, own_out = w_in[0], w_out[0]
    gates = gate_weights.T
    oth_in = hold(lax.ppermute(own_in, "yl", SWAP), HOLD_FLOPS)
    outgoing, target = dispatch(expert_ids.T, gates, tokens, d_out, experts)
    arrived = exchange(outgoing.reshape(experts, 4 * width, LANES), groups)
    oth_out = lax.ppermute(own_out, "yl", SWAP)
    own_in, own_out, oth_in = lax.optimization_barrier((own_in, own_out, oth_in))
    near = [own_in, own_out, lax.ppermute(own_in, "core", SWAP), lax.ppermute(own_out, "core", SWAP)]
    far = [oth_in, oth_out, lax.ppermute(oth_in, "core", SWAP), lax.ppermute(oth_out, "core", SWAP)]
    arrived, *blocks = lax.optimization_barrier((arrived, *near, *far))
    rows = arrived.reshape(slots, 2 * model)
    own_gi, own_go, peer_gi, peer_go, far_gi, far_go, send_gi, send_go, back = run_experts(rows, blocks)

    def add(a, b):
        return (a.astype(f32) + b.astype(f32)).astype(bf16)

    sum_in = add(far_gi, lax.ppermute(send_gi, "core", SWAP))
    came_in = hold(lax.ppermute(sum_in, "yl", SWAP), HOLD_FLOPS)
    back, send_go, _ = lax.optimization_barrier((back, send_go, sum_in))
    returned = exchange(back, groups)
    got_go = hold(lax.ppermute(send_go, "core", SWAP), HOLD_FLOPS)
    sum_out = add(far_go, got_go)
    sum_out, peer_gi, peer_go = lax.optimization_barrier((sum_out, peer_gi, peer_go))
    came_out = lax.ppermute(sum_out, "yl", SWAP)
    near_in = lax.ppermute(peer_gi, "core", SWAP)
    near_out = lax.ppermute(peer_go, "core", SWAP)
    d_first = finish(own_gi, near_in, came_in, True)
    returned, d_first = lax.optimization_barrier((returned, d_first))
    d_tokens, d_gates = combine(target, returned, gates, model)
    came_out, d_tokens, d_gates = lax.optimization_barrier((came_out, d_tokens, d_gates))
    d_second = finish(own_go, near_out, came_out, False)
    return (d_tokens, d_gates.T, d_first[None], d_second[None])


def solution(mesh):
    dp, expert = mesh.devices.shape
    pairs = expert // 4
    fine = Mesh(np.asarray(mesh.devices).reshape(dp, pairs, 2, 2), AXES)
    number = np.arange(dp * expert).reshape(dp, pairs, 2, 2)
    near = np.arange(pairs) >= pairs // 2
    groups = [
        [int(number[i, k, int(near[k]) ^ side, c]) for i in range(dp) for k in range(pairs)]
        for side in range(2)
        for c in range(2)
    ]
    flat, block = P(AXES, None), P(AXES, None, None)
    return jax.shard_map(
        functools.partial(on_device, groups),
        mesh=fine,
        in_specs=(flat, flat, flat, flat, block, block),
        out_specs=(flat, flat, block, block),
        check_vma=False,
    )
```

```python
import functools

import jax
import jax.numpy as jnp
import numpy as np
from jax import lax
from jax.experimental import pallas as pl
from jax.experimental.pallas import tpu as pltpu
from jax.sharding import Mesh
from jax.sharding import PartitionSpec as P

TOPK = 4
LANES = 128
AXES = ("dp", "yh", "yl", "core")
GATE_ROWS = 8
HOLD_FLOPS = int(3e10)
SWAP = [(0, 1), (1, 0)]
f32, bf16 = jnp.float32, jnp.bfloat16


def dispatch_kernel(
    ids_ref, gates_ref, tok_ref, dout_ref, out_ref, target_ref, count_ref, tok_lines, dout_lines
):
    tokens, model = tok_ref.shape
    width = model // LANES
    for j in range(width):
        part = slice(j * LANES, (j + 1) * LANES)
        tok_lines[pl.ds(j, tokens, stride=width), :] = tok_ref[:, part].astype(f32)
        dout_lines[pl.ds(j, tokens, stride=width), :] = dout_ref[:, part].astype(f32)
    out_ref[...] = jnp.zeros_like(out_ref)

    def clear(i, carry):
        count_ref[i] = 0
        return carry

    lax.fori_loop(0, count_ref.shape[0], clear, 0, unroll=8)

    def place(t, carry):
        lines = pl.ds(pl.multiple_of(t * width, width), width)
        row = tok_lines[lines, :].astype(bf16)
        grad = dout_lines[lines, :]
        for k in range(TOPK):
            e = ids_ref[k, t]
            slot = count_ref[e]
            count_ref[e] = slot + 1
            at = 2 * e + slot
            target_ref[k, t] = at
            out_ref[at, 0:width, :] = row
            out_ref[at, width : 2 * width, :] = (grad * gates_ref[k, t]).astype(bf16)
        return carry

    lax.fori_loop(0, tokens, place, 0)


def dispatch(ids, gates, tokens, d_out, experts):
    rows, model = tokens.shape
    width = model // LANES
    smem = pl.BlockSpec(memory_space=pltpu.SMEM)
    vmem = pl.BlockSpec(memory_space=pltpu.VMEM)
    return pl.pallas_call(
        dispatch_kernel,
        out_shape=(
            jax.ShapeDtypeStruct((2 * experts, 2 * width, LANES), bf16),
            jax.ShapeDtypeStruct((TOPK, rows), jnp.int32),
        ),
        in_specs=[smem, smem, vmem, vmem],
        out_specs=(vmem, smem),
        scratch_shapes=[
            pltpu.SMEM((experts,), jnp.int32),
            pltpu.VMEM((rows * width, LANES), f32),
            pltpu.VMEM((rows * width, LANES), f32),
        ],
        name="dispatch",
    )(ids, gates, tokens, d_out)


def hold(x, flops):
    anywhere = pl.BlockSpec(memory_space=pl.ANY)
    return pl.pallas_call(
        lambda x_ref, y_ref: None,
        out_shape=jax.ShapeDtypeStruct(x.shape, x.dtype),
        in_specs=[anywhere],
        out_specs=anywhere,
        input_output_aliases={0: 0},
        cost_estimate=pl.CostEstimate(flops=flops, bytes_accessed=0, transcendentals=0),
        name="hold",
    )(x)


def combine_kernel(target_ref, back_ref, gates_ref, dx_ref, gate_ref, dx_rows, gate_rows):
    tokens, model = dx_ref.shape
    width = model // LANES
    lane = lax.broadcasted_iota(jnp.int32, (1, LANES), 1)

    def total(t, carry):
        acc = jnp.zeros((width, LANES), f32)
        gate = jnp.zeros((1, LANES), f32)
        for k in range(TOPK):
            at = target_ref[k, t]
            e, slot = lax.shift_right_logical(at, 1), lax.bitwise_and(at, 1)
            first = pl.multiple_of(slot * width, width)
            acc += back_ref[e, pl.ds(first, width), :].astype(f32)
            extra = back_ref[e, 2 * width : 2 * width + GATE_ROWS, :].astype(f32)
            pair = jnp.where(slot == 0, extra[0:2, :], extra[2:4, :])
            gate = jnp.where(lane == k, pair[0:1, :] + pair[1:2, :], gate)
        dx_rows[pl.ds(pl.multiple_of(t * width, width), width), :] = acc
        gate_rows[pl.ds(t, 1), :] = gate
        return carry

    lax.fori_loop(0, tokens, total, 0)
    for j in range(width):
        part = dx_rows[pl.ds(j, tokens, stride=width), :]
        dx_ref[:, j * LANES : (j + 1) * LANES] = part.astype(bf16)
    gate_ref[...] = gate_rows[...].T[:TOPK, :] / gates_ref[...]


def combine(target, back, gates, model):
    tokens = gates.shape[1]
    vmem = pl.BlockSpec(memory_space=pltpu.VMEM)
    return pl.pallas_call(
        combine_kernel,
        out_shape=(
            jax.ShapeDtypeStruct((tokens, model), bf16),
            jax.ShapeDtypeStruct(gates.shape, f32),
        ),
        in_specs=[pl.BlockSpec(memory_space=pltpu.SMEM), vmem, vmem],
        out_specs=(vmem, vmem),
        scratch_shapes=[
            pltpu.VMEM((tokens * model // LANES, LANES), f32),
            pltpu.VMEM((tokens, LANES), f32),
        ],
        name="combine",
    )(target, back, gates)


def dot(a, b, ca, cb):
    return lax.dot_general(a, b, (((ca,), (cb,)), ((), ())), preferred_element_type=f32)


def experts_kernel(rows_hbm, *refs):
    blocks, stores_to, back_ref = refs[:10], refs[10:18], refs[18]
    rows, ins, outs, grads, total, lines, in_sems, out_sems = refs[19:]
    hidden, model = outs.shape[1], outs.shape[2]
    slots, width = rows.shape[0], model // LANES
    experts = slots // 2
    half = hidden // 2
    loads = [pltpu.make_async_copy(rows_hbm, rows, in_sems.at[0])]
    places = []
    for q in range(4):
        places.append((q, ins.at[q]))
        if q < 2:
            places.append((q, outs.at[q]))
        else:
            places += [(q, outs.at[q, pl.ds(0, half), :]), (q, outs.at[q, pl.ds(half, half), :])]
    loads += [
        pltpu.make_async_copy(block, place, in_sems.at[1 + n])
        for n, (block, (_, place)) in enumerate(zip(blocks, places))
    ]
    stores = []
    for q in range(4):
        cut = hidden if q < 2 else hidden + half
        first = pltpu.make_async_copy(grads.at[q, pl.ds(0, cut), :], stores_to[2 * q], out_sems.at[2 * q])
        second = pltpu.make_async_copy(
            grads.at[q, pl.ds(cut, 2 * hidden - cut), :], stores_to[2 * q + 1], out_sems.at[2 * q + 1]
        )
        stores += [first, second]
    for load in loads:
        load.start()
    loads[0].wait()
    gate = jnp.zeros((slots, 1), f32)
    for q in range(4):
        for load, (user, _) in zip(loads[1:], places):
            if user == q:
                load.wait()
        preact = dot(rows[:, :model], ins[q], 1, 0)
        pulled = dot(rows[:, model:], outs[q], 1, 1)
        sig = jax.nn.sigmoid(preact)
        act = preact * sig
        d_pre = (pulled * sig * (1.0 + preact * (1.0 - sig))).astype(bf16)
        gate += jnp.sum(act * pulled, axis=1, keepdims=True)
        act = act.astype(bf16)
        grads[q, :hidden, :] = dot(d_pre, rows[:, :model], 0, 0).astype(bf16)
        grads[q, hidden:, :] = dot(act, rows[:, model:], 0, 0).astype(bf16)
        stores[2 * q].start()
        stores[2 * q + 1].start()
        part = dot(d_pre, ins[q], 1, 1)
        total[...] = part if q == 0 else total[...] + part
    for j in range(width):
        lines[pl.ds(j, slots, stride=width), :] = total[:, j * LANES : (j + 1) * LANES]
    back_ref[:, : 2 * width, :] = lines[...].astype(bf16).reshape(experts, 2 * width, LANES)
    gate = jnp.broadcast_to(gate, (slots, LANES))
    high = gate.astype(bf16)
    low = (gate - high.astype(f32)).astype(bf16)
    row = lax.broadcasted_iota(jnp.int32, (experts * GATE_ROWS, slots), 0)
    slot = lax.broadcasted_iota(jnp.int32, (experts * GATE_ROWS, slots), 1)
    place = row - (slot >> 1) * GATE_ROWS - 2 * (slot & 1)
    spread = dot((place == 0).astype(bf16), high, 1, 0) + dot((place == 1).astype(bf16), low, 1, 0)
    back_ref[:, 2 * width :, :] = spread.astype(bf16).reshape(experts, GATE_ROWS, LANES)
    for store in stores:
        store.wait()


def run_experts(rows, blocks):
    slots, model = rows.shape[0], rows.shape[1] // 2
    hidden = blocks[1].shape[0]
    width = model // LANES
    anywhere = pl.BlockSpec(memory_space=pl.ANY)
    vmem = pl.BlockSpec(memory_space=pltpu.VMEM)
    return pl.pallas_call(
        experts_kernel,
        out_shape=tuple(
            jax.ShapeDtypeStruct((r, model), bf16)
            for r in [hidden] * 4 + [hidden + hidden // 2, hidden // 2] * 2
        )
        + (jax.ShapeDtypeStruct((slots // 2, 2 * width + GATE_ROWS, LANES), bf16),),
        in_specs=[anywhere] * 11,
        out_specs=(anywhere,) * 8 + (vmem,),
        scratch_shapes=[
            pltpu.VMEM(rows.shape, bf16),
            pltpu.VMEM((4, model, hidden), bf16),
            pltpu.VMEM((4, hidden, model), bf16),
            pltpu.VMEM((4, 2 * hidden, model), bf16),
            pltpu.VMEM((slots, model), f32),
            pltpu.VMEM((slots * width, LANES), f32),
            pltpu.SemaphoreType.DMA((11,)),
            pltpu.SemaphoreType.DMA((8,)),
        ],
        cost_estimate=pl.CostEstimate(
            flops=4 * 5 * 2 * slots * model * hidden,
            bytes_accessed=2 * (rows.size + 16 * hidden * model),
            transcendentals=0,
        ),
        name="experts",
    )(rows, *blocks)


def finish_first_kernel(own_ref, peer_ref, came_ref, out_ref):
    total = own_ref[...].astype(f32) + peer_ref[...].astype(f32) + came_ref[...].astype(f32)
    out_ref[...] = total.T.astype(bf16)


def finish_second_kernel(own_ref, peer_ref, upper_ref, lower_ref, out_ref):
    half = upper_ref.shape[0]
    total = own_ref[...].astype(f32) + peer_ref[...].astype(f32)
    out_ref[:half, :] = (total[:half, :] + upper_ref[...].astype(f32)).astype(bf16)
    out_ref[half:, :] = (total[half:, :] + lower_ref[...].astype(f32)).astype(bf16)


def finish_first(own, peer, came):
    hidden, model = own.shape
    part = pl.BlockSpec((hidden, 512), lambda j: (0, j))
    return pl.pallas_call(
        finish_first_kernel,
        grid=(model // 512,),
        out_shape=jax.ShapeDtypeStruct((model, hidden), bf16),
        in_specs=[part] * 3,
        out_specs=pl.BlockSpec((512, hidden), lambda j: (j, 0)),
        name="finish_first",
    )(own, peer, came)


def finish_second(own, peer, came, rest):
    hidden, model = own.shape
    half = hidden // 2
    part = pl.BlockSpec((hidden, 512), lambda j: (0, j))
    return pl.pallas_call(
        finish_second_kernel,
        grid=(model // 512,),
        out_shape=jax.ShapeDtypeStruct((hidden, model), bf16),
        in_specs=[
            part,
            part,
            pl.BlockSpec((half, 512), lambda j: (2, j)),
            pl.BlockSpec((half, 512), lambda j: (0, j)),
        ],
        out_specs=part,
        name="finish_second",
    )(own, peer, came, rest)


def exchange(x, groups):
    return lax.all_to_all(
        x, AXES, split_axis=0, concat_axis=0, axis_index_groups=groups, tiled=True
    )


def on_device(groups, tokens, d_out, expert_ids, gate_weights, w_in, w_out):
    tok_rows, model = tokens.shape
    width = model // LANES
    experts = len(groups[0])
    slots = 2 * experts
    own_in, own_out = w_in[0], w_out[0]
    gates = gate_weights.T
    half = own_out.shape[0] // 2
    oth_in = hold(lax.ppermute(own_in, "yl", SWAP), HOLD_FLOPS)
    oth_upper = hold(lax.ppermute(own_out[:half], "yl", SWAP), HOLD_FLOPS)
    outgoing, target = dispatch(expert_ids.T, gates, tokens, d_out, experts)
    arrived = exchange(outgoing.reshape(experts, 4 * width, LANES), groups)
    own_in, own_out, oth_in = lax.optimization_barrier((own_in, own_out, oth_in))
    oth_lower = lax.ppermute(own_out[half:], "yl", SWAP)
    near = [own_in, own_out, lax.ppermute(own_in, "core", SWAP), lax.ppermute(own_out, "core", SWAP)]
    far = [oth_in, oth_upper, oth_lower]
    far += [lax.ppermute(w, "core", SWAP) for w in far]
    arrived, *blocks = lax.optimization_barrier((arrived, *near, *far))
    rows = arrived.reshape(slots, 2 * model)
    own_gi, own_go, peer_gi, peer_go, far_a, far_b, send_a, send_b, back = run_experts(rows, blocks)

    def add(a, b):
        return (a.astype(f32) + b.astype(f32)).astype(bf16)

    sum_a = add(far_a, lax.ppermute(send_a, "core", SWAP))
    came_a = hold(lax.ppermute(sum_a, "yl", SWAP), HOLD_FLOPS)
    back, send_b, _ = lax.optimization_barrier((back, send_b, sum_a))
    returned = exchange(back, groups)
    got_b = hold(lax.ppermute(send_b, "core", SWAP), HOLD_FLOPS)
    sum_b = add(far_b, got_b)
    sum_b, peer_gi, peer_go = lax.optimization_barrier((sum_b, peer_gi, peer_go))
    came_b = lax.ppermute(sum_b, "yl", SWAP)
    near_in = lax.ppermute(peer_gi, "core", SWAP)
    near_out = lax.ppermute(peer_go, "core", SWAP)
    d_first = finish_first(own_gi, near_in, came_a)
    returned, d_first = lax.optimization_barrier((returned, d_first))
    d_tokens, d_gates = combine(target, returned, gates, model)
    came_b, d_tokens, d_gates = lax.optimization_barrier((came_b, d_tokens, d_gates))
    d_second = finish_second(own_go, near_out, came_a, came_b)
    return (d_tokens, d_gates.T, d_first[None], d_second[None])


def solution(mesh):
    dp, expert = mesh.devices.shape
    pairs = expert // 4
    fine = Mesh(np.asarray(mesh.devices).reshape(dp, pairs, 2, 2), AXES)
    number = np.arange(dp * expert).reshape(dp, pairs, 2, 2)
    near = np.arange(pairs) >= pairs // 2
    groups = [
        [int(number[i, k, int(near[k]) ^ side, c]) for i in range(dp) for k in range(pairs)]
        for side in range(2)
        for c in range(2)
    ]
    flat, block = P(AXES, None), P(AXES, None, None)
    return jax.shard_map(
        functools.partial(on_device, groups),
        mesh=fine,
        in_specs=(flat, flat, flat, flat, block, block),
        out_specs=(flat, flat, block, block),
        check_vma=False,
    )
```

```python
import functools

import jax
import jax.numpy as jnp
import numpy as np
from jax import lax
from jax.experimental import pallas as pl
from jax.experimental.pallas import tpu as pltpu
from jax.sharding import Mesh
from jax.sharding import PartitionSpec as P

TOPK = 4
LANES = 128
AXES = ("dp", "yh", "yl", "core")
GATE_ROWS = 8
AHEAD_OUT = 192
AHEAD_GRAD = 64
HOLD_FLOPS = int(3e10)
SWAP = [(0, 1), (1, 0)]
f32, bf16 = jnp.float32, jnp.bfloat16


def dispatch_kernel(
    ids_ref, gates_ref, tok_ref, dout_ref, out_ref, target_ref, count_ref, tok_lines, dout_lines
):
    tokens, model = tok_ref.shape
    width = model // LANES
    for j in range(width):
        part = slice(j * LANES, (j + 1) * LANES)
        tok_lines[pl.ds(j, tokens, stride=width), :] = tok_ref[:, part].astype(f32)
        dout_lines[pl.ds(j, tokens, stride=width), :] = dout_ref[:, part].astype(f32)
    out_ref[...] = jnp.zeros_like(out_ref)

    def clear(i, carry):
        count_ref[i] = 0
        return carry

    lax.fori_loop(0, count_ref.shape[0], clear, 0, unroll=8)

    def place(t, carry):
        lines = pl.ds(pl.multiple_of(t * width, width), width)
        row = tok_lines[lines, :].astype(bf16)
        grad = dout_lines[lines, :]
        for k in range(TOPK):
            e = ids_ref[k, t]
            slot = count_ref[e]
            count_ref[e] = slot + 1
            at = 2 * e + slot
            target_ref[k, t] = at
            out_ref[at, 0:width, :] = row
            out_ref[at, width : 2 * width, :] = (grad * gates_ref[k, t]).astype(bf16)
        return carry

    lax.fori_loop(0, tokens, place, 0)


def dispatch(ids, gates, tokens, d_out, experts):
    rows, model = tokens.shape
    width = model // LANES
    smem = pl.BlockSpec(memory_space=pltpu.SMEM)
    vmem = pl.BlockSpec(memory_space=pltpu.VMEM)
    return pl.pallas_call(
        dispatch_kernel,
        out_shape=(
            jax.ShapeDtypeStruct((2 * experts, 2 * width, LANES), bf16),
            jax.ShapeDtypeStruct((TOPK, rows), jnp.int32),
        ),
        in_specs=[smem, smem, vmem, vmem],
        out_specs=(vmem, smem),
        scratch_shapes=[
            pltpu.SMEM((experts,), jnp.int32),
            pltpu.VMEM((rows * width, LANES), f32),
            pltpu.VMEM((rows * width, LANES), f32),
        ],
        name="dispatch",
    )(ids, gates, tokens, d_out)


def hold(x, flops):
    anywhere = pl.BlockSpec(memory_space=pl.ANY)
    return pl.pallas_call(
        lambda x_ref, y_ref: None,
        out_shape=jax.ShapeDtypeStruct(x.shape, x.dtype),
        in_specs=[anywhere],
        out_specs=anywhere,
        input_output_aliases={0: 0},
        cost_estimate=pl.CostEstimate(flops=flops, bytes_accessed=0, transcendentals=0),
        name="hold",
    )(x)


def combine_kernel(target_ref, back_ref, gates_ref, dx_ref, gate_ref, dx_rows, gate_rows):
    tokens, model = dx_ref.shape
    width = model // LANES
    lane = lax.broadcasted_iota(jnp.int32, (1, LANES), 1)

    def total(t, carry):
        acc = jnp.zeros((width, LANES), f32)
        gate = jnp.zeros((1, LANES), f32)
        for k in range(TOPK):
            at = target_ref[k, t]
            e, slot = lax.shift_right_logical(at, 1), lax.bitwise_and(at, 1)
            first = pl.multiple_of(slot * width, width)
            acc += back_ref[e, pl.ds(first, width), :].astype(f32)
            extra = back_ref[e, 2 * width : 2 * width + GATE_ROWS, :].astype(f32)
            pair = jnp.where(slot == 0, extra[0:2, :], extra[2:4, :])
            gate = jnp.where(lane == k, pair[0:1, :] + pair[1:2, :], gate)
        dx_rows[pl.ds(pl.multiple_of(t * width, width), width), :] = acc
        gate_rows[pl.ds(t, 1), :] = gate
        return carry

    lax.fori_loop(0, tokens, total, 0)
    for j in range(width):
        part = dx_rows[pl.ds(j, tokens, stride=width), :]
        dx_ref[:, j * LANES : (j + 1) * LANES] = part.astype(bf16)
    gate_ref[...] = gate_rows[...].T[:TOPK, :] / gates_ref[...]


def combine(target, back, gates, model):
    tokens = gates.shape[1]
    vmem = pl.BlockSpec(memory_space=pltpu.VMEM)
    return pl.pallas_call(
        combine_kernel,
        out_shape=(
            jax.ShapeDtypeStruct((tokens, model), bf16),
            jax.ShapeDtypeStruct(gates.shape, f32),
        ),
        in_specs=[pl.BlockSpec(memory_space=pltpu.SMEM), vmem, vmem],
        out_specs=(vmem, vmem),
        scratch_shapes=[
            pltpu.VMEM((tokens * model // LANES, LANES), f32),
            pltpu.VMEM((tokens, LANES), f32),
        ],
        name="combine",
    )(target, back, gates)


def dot(a, b, ca, cb):
    return lax.dot_general(a, b, (((ca,), (cb,)), ((), ())), preferred_element_type=f32)


def experts_kernel(rows_hbm, *refs):
    blocks, stores_to, back_ref = refs[:10], refs[10:18], refs[18]
    rows, ins, outs, grads, total, lines, in_sems, out_sems = refs[19:]
    hidden, model = outs.shape[1], outs.shape[2]
    slots, width = rows.shape[0], model // LANES
    experts = slots // 2
    loads = [pltpu.make_async_copy(rows_hbm, rows, in_sems.at[0])]
    places = []
    for q in range(4):
        places.append((q, ins.at[q]))
        if q < 2:
            places.append((q, outs.at[q]))
        else:
            ahead, behind = pl.ds(0, AHEAD_OUT), pl.ds(AHEAD_OUT, hidden - AHEAD_OUT)
            places += [(q, outs.at[q, ahead, :]), (q, outs.at[q, behind, :])]
    loads += [
        pltpu.make_async_copy(block, place, in_sems.at[1 + n])
        for n, (block, (_, place)) in enumerate(zip(blocks, places))
    ]
    stores = []
    for q in range(4):
        cut = hidden if q < 2 else hidden + AHEAD_GRAD
        first = pltpu.make_async_copy(grads.at[q, pl.ds(0, cut), :], stores_to[2 * q], out_sems.at[2 * q])
        second = pltpu.make_async_copy(
            grads.at[q, pl.ds(cut, 2 * hidden - cut), :], stores_to[2 * q + 1], out_sems.at[2 * q + 1]
        )
        stores += [first, second]
    for load in loads:
        load.start()
    loads[0].wait()
    gate = jnp.zeros((slots, 1), f32)
    for q in range(4):
        for load, (user, _) in zip(loads[1:], places):
            if user == q:
                load.wait()
        preact = dot(rows[:, :model], ins[q], 1, 0)
        pulled = dot(rows[:, model:], outs[q], 1, 1)
        sig = jax.nn.sigmoid(preact)
        act = preact * sig
        d_pre = (pulled * sig * (1.0 + preact * (1.0 - sig))).astype(bf16)
        gate += jnp.sum(act * pulled, axis=1, keepdims=True)
        act = act.astype(bf16)
        grads[q, :hidden, :] = dot(d_pre, rows[:, :model], 0, 0).astype(bf16)
        grads[q, hidden:, :] = dot(act, rows[:, model:], 0, 0).astype(bf16)
        stores[2 * q].start()
        stores[2 * q + 1].start()
        part = dot(d_pre, ins[q], 1, 1)
        total[...] = part if q == 0 else total[...] + part
    for j in range(width):
        lines[pl.ds(j, slots, stride=width), :] = total[:, j * LANES : (j + 1) * LANES]
    back_ref[:, : 2 * width, :] = lines[...].astype(bf16).reshape(experts, 2 * width, LANES)
    gate = jnp.broadcast_to(gate, (slots, LANES))
    high = gate.astype(bf16)
    low = (gate - high.astype(f32)).astype(bf16)
    row = lax.broadcasted_iota(jnp.int32, (experts * GATE_ROWS, slots), 0)
    slot = lax.broadcasted_iota(jnp.int32, (experts * GATE_ROWS, slots), 1)
    place = row - (slot >> 1) * GATE_ROWS - 2 * (slot & 1)
    spread = dot((place == 0).astype(bf16), high, 1, 0) + dot((place == 1).astype(bf16), low, 1, 0)
    back_ref[:, 2 * width :, :] = spread.astype(bf16).reshape(experts, GATE_ROWS, LANES)
    for store in stores:
        store.wait()


def run_experts(rows, blocks):
    slots, model = rows.shape[0], rows.shape[1] // 2
    hidden = blocks[1].shape[0]
    width = model // LANES
    anywhere = pl.BlockSpec(memory_space=pl.ANY)
    vmem = pl.BlockSpec(memory_space=pltpu.VMEM)
    return pl.pallas_call(
        experts_kernel,
        out_shape=tuple(
            jax.ShapeDtypeStruct((r, model), bf16)
            for r in [hidden] * 4 + [hidden + AHEAD_GRAD, hidden - AHEAD_GRAD] * 2
        )
        + (jax.ShapeDtypeStruct((slots // 2, 2 * width + GATE_ROWS, LANES), bf16),),
        in_specs=[anywhere] * 11,
        out_specs=(anywhere,) * 8 + (vmem,),
        scratch_shapes=[
            pltpu.VMEM(rows.shape, bf16),
            pltpu.VMEM((4, model, hidden), bf16),
            pltpu.VMEM((4, hidden, model), bf16),
            pltpu.VMEM((4, 2 * hidden, model), bf16),
            pltpu.VMEM((slots, model), f32),
            pltpu.VMEM((slots * width, LANES), f32),
            pltpu.SemaphoreType.DMA((11,)),
            pltpu.SemaphoreType.DMA((8,)),
        ],
        cost_estimate=pl.CostEstimate(
            flops=4 * 5 * 2 * slots * model * hidden,
            bytes_accessed=2 * (rows.size + 16 * hidden * model),
            transcendentals=0,
        ),
        name="experts",
    )(rows, *blocks)


def finish_first_kernel(own_ref, peer_ref, came_ref, out_ref):
    total = own_ref[...].astype(f32) + peer_ref[...].astype(f32) + came_ref[...].astype(f32)
    out_ref[...] = total.T.astype(bf16)


def finish_second_kernel(own_ref, peer_ref, upper_ref, lower_ref, out_ref):
    half = upper_ref.shape[0]
    total = own_ref[...].astype(f32) + peer_ref[...].astype(f32)
    out_ref[:half, :] = (total[:half, :] + upper_ref[...].astype(f32)).astype(bf16)
    out_ref[half:, :] = (total[half:, :] + lower_ref[...].astype(f32)).astype(bf16)


def finish_first(own, peer, came):
    hidden, model = own.shape
    part = pl.BlockSpec((hidden, 512), lambda j: (0, j))
    return pl.pallas_call(
        finish_first_kernel,
        grid=(model // 512,),
        out_shape=jax.ShapeDtypeStruct((model, hidden), bf16),
        in_specs=[part] * 3,
        out_specs=pl.BlockSpec((512, hidden), lambda j: (j, 0)),
        name="finish_first",
    )(own, peer, came)


def finish_second(own, peer, came, rest):
    hidden, model = own.shape
    part = pl.BlockSpec((hidden, 1024), lambda j: (0, j))
    return pl.pallas_call(
        finish_second_kernel,
        grid=(model // 1024,),
        out_shape=jax.ShapeDtypeStruct((hidden, model), bf16),
        in_specs=[
            part,
            part,
            pl.BlockSpec((AHEAD_GRAD, 1024), lambda j: (hidden // AHEAD_GRAD, j)),
            pl.BlockSpec((hidden - AHEAD_GRAD, 1024), lambda j: (0, j)),
        ],
        out_specs=part,
        name="finish_second",
    )(own, peer, came, rest)


def exchange(x, groups):
    return lax.all_to_all(
        x, AXES, split_axis=0, concat_axis=0, axis_index_groups=groups, tiled=True
    )


def on_device(groups, tokens, d_out, expert_ids, gate_weights, w_in, w_out):
    tok_rows, model = tokens.shape
    width = model // LANES
    experts = len(groups[0])
    slots = 2 * experts
    own_in, own_out = w_in[0], w_out[0]
    gates = gate_weights.T
    oth_in = hold(lax.ppermute(own_in, "yl", SWAP), HOLD_FLOPS)
    oth_upper = hold(lax.ppermute(own_out[:AHEAD_OUT], "yl", SWAP), HOLD_FLOPS)
    outgoing, target = dispatch(expert_ids.T, gates, tokens, d_out, experts)
    arrived = exchange(outgoing.reshape(experts, 4 * width, LANES), groups)
    own_in, own_out, oth_in = lax.optimization_barrier((own_in, own_out, oth_in))
    oth_lower = hold(lax.ppermute(own_out[AHEAD_OUT:], "yl", SWAP), HOLD_FLOPS)
    near = [own_in, own_out, lax.ppermute(own_in, "core", SWAP), lax.ppermute(own_out, "core", SWAP)]
    far = [oth_in, oth_upper, oth_lower]
    far += [lax.ppermute(w, "core", SWAP) for w in far]
    arrived, *blocks = lax.optimization_barrier((arrived, *near, *far))
    rows = arrived.reshape(slots, 2 * model)
    own_gi, own_go, peer_gi, peer_go, far_a, far_b, send_a, send_b, back = run_experts(rows, blocks)

    def add(a, b):
        return (a.astype(f32) + b.astype(f32)).astype(bf16)

    sum_a = add(far_a, lax.ppermute(send_a, "core", SWAP))
    came_a = hold(lax.ppermute(sum_a, "yl", SWAP), HOLD_FLOPS)
    back, send_b, _ = lax.optimization_barrier((back, send_b, sum_a))
    returned = exchange(back, groups)
    got_b = hold(lax.ppermute(send_b, "core", SWAP), HOLD_FLOPS)
    sum_b = add(far_b, got_b)
    sum_b, peer_gi, peer_go = lax.optimization_barrier((sum_b, peer_gi, peer_go))
    came_b = lax.ppermute(sum_b, "yl", SWAP)
    near_in = lax.ppermute(peer_gi, "core", SWAP)
    near_out = lax.ppermute(peer_go, "core", SWAP)
    d_first = finish_first(own_gi, near_in, came_a)
    returned, d_first = lax.optimization_barrier((returned, d_first))
    d_tokens, d_gates = combine(target, returned, gates, model)
    came_b, d_tokens, d_gates = lax.optimization_barrier((came_b, d_tokens, d_gates))
    d_second = finish_second(own_go, near_out, came_a, came_b)
    return (d_tokens, d_gates.T, d_first[None], d_second[None])


def solution(mesh):
    dp, expert = mesh.devices.shape
    pairs = expert // 4
    fine = Mesh(np.asarray(mesh.devices).reshape(dp, pairs, 2, 2), AXES)
    number = np.arange(dp * expert).reshape(dp, pairs, 2, 2)
    near = np.arange(pairs) >= pairs // 2
    groups = [
        [int(number[i, k, int(near[k]) ^ side, c]) for i in range(dp) for k in range(pairs)]
        for side in range(2)
        for c in range(2)
    ]
    flat, block = P(AXES, None), P(AXES, None, None)
    return jax.shard_map(
        functools.partial(on_device, groups),
        mesh=fine,
        in_specs=(flat, flat, flat, flat, block, block),
        out_specs=(flat, flat, block, block),
        check_vma=False,
    )
```

```python
import functools

import jax
import jax.numpy as jnp
import numpy as np
from jax import lax
from jax.experimental import pallas as pl
from jax.experimental.pallas import tpu as pltpu
from jax.sharding import Mesh
from jax.sharding import PartitionSpec as P

TOPK = 4
LANES = 128
AXES = ("dp", "yh", "yl", "core")
GATE_ROWS = 8
AHEAD_OUT = 192
AHEAD_GRAD = 128
HOLD_FLOPS = int(3e10)
SWAP = [(0, 1), (1, 0)]
f32, bf16 = jnp.float32, jnp.bfloat16


def dispatch_kernel(
    ids_ref, gates_ref, tok_ref, dout_ref, out_ref, target_ref, count_ref, tok_lines, dout_lines
):
    tokens, model = tok_ref.shape
    width = model // LANES
    for j in range(width):
        part = slice(j * LANES, (j + 1) * LANES)
        tok_lines[pl.ds(j, tokens, stride=width), :] = tok_ref[:, part].astype(f32)
        dout_lines[pl.ds(j, tokens, stride=width), :] = dout_ref[:, part].astype(f32)
    out_ref[...] = jnp.zeros_like(out_ref)

    def clear(i, carry):
        count_ref[i] = 0
        return carry

    lax.fori_loop(0, count_ref.shape[0], clear, 0, unroll=8)

    def place(t, carry):
        lines = pl.ds(pl.multiple_of(t * width, width), width)
        row = tok_lines[lines, :].astype(bf16)
        grad = dout_lines[lines, :]
        for k in range(TOPK):
            e = ids_ref[k, t]
            slot = count_ref[e]
            count_ref[e] = slot + 1
            at = 2 * e + slot
            target_ref[k, t] = at
            out_ref[at, 0:width, :] = row
            out_ref[at, width : 2 * width, :] = (grad * gates_ref[k, t]).astype(bf16)
        return carry

    lax.fori_loop(0, tokens, place, 0)


def dispatch(ids, gates, tokens, d_out, experts):
    rows, model = tokens.shape
    width = model // LANES
    smem = pl.BlockSpec(memory_space=pltpu.SMEM)
    vmem = pl.BlockSpec(memory_space=pltpu.VMEM)
    return pl.pallas_call(
        dispatch_kernel,
        out_shape=(
            jax.ShapeDtypeStruct((2 * experts, 2 * width, LANES), bf16),
            jax.ShapeDtypeStruct((TOPK, rows), jnp.int32),
        ),
        in_specs=[smem, smem, vmem, vmem],
        out_specs=(vmem, smem),
        scratch_shapes=[
            pltpu.SMEM((experts,), jnp.int32),
            pltpu.VMEM((rows * width, LANES), f32),
            pltpu.VMEM((rows * width, LANES), f32),
        ],
        name="dispatch",
    )(ids, gates, tokens, d_out)


def hold(x, flops):
    anywhere = pl.BlockSpec(memory_space=pl.ANY)
    return pl.pallas_call(
        lambda x_ref, y_ref: None,
        out_shape=jax.ShapeDtypeStruct(x.shape, x.dtype),
        in_specs=[anywhere],
        out_specs=anywhere,
        input_output_aliases={0: 0},
        cost_estimate=pl.CostEstimate(flops=flops, bytes_accessed=0, transcendentals=0),
        name="hold",
    )(x)


def combine_kernel(target_ref, back_ref, gates_ref, dx_ref, gate_ref, dx_rows, gate_rows):
    tokens, model = dx_ref.shape
    width = model // LANES
    lane = lax.broadcasted_iota(jnp.int32, (1, LANES), 1)

    def total(t, carry):
        acc = jnp.zeros((width, LANES), f32)
        gate = jnp.zeros((1, LANES), f32)
        for k in range(TOPK):
            at = target_ref[k, t]
            e, slot = lax.shift_right_logical(at, 1), lax.bitwise_and(at, 1)
            first = pl.multiple_of(slot * width, width)
            acc += back_ref[e, pl.ds(first, width), :].astype(f32)
            extra = back_ref[e, 2 * width : 2 * width + GATE_ROWS, :].astype(f32)
            pair = jnp.where(slot == 0, extra[0:2, :], extra[2:4, :])
            gate = jnp.where(lane == k, pair[0:1, :] + pair[1:2, :], gate)
        dx_rows[pl.ds(pl.multiple_of(t * width, width), width), :] = acc
        gate_rows[pl.ds(t, 1), :] = gate
        return carry

    lax.fori_loop(0, tokens, total, 0)
    for j in range(width):
        part = dx_rows[pl.ds(j, tokens, stride=width), :]
        dx_ref[:, j * LANES : (j + 1) * LANES] = part.astype(bf16)
    gate_ref[...] = gate_rows[...].T[:TOPK, :] / gates_ref[...]


def combine(target, back, gates, model):
    tokens = gates.shape[1]
    vmem = pl.BlockSpec(memory_space=pltpu.VMEM)
    return pl.pallas_call(
        combine_kernel,
        out_shape=(
            jax.ShapeDtypeStruct((tokens, model), bf16),
            jax.ShapeDtypeStruct(gates.shape, f32),
        ),
        in_specs=[pl.BlockSpec(memory_space=pltpu.SMEM), vmem, vmem],
        out_specs=(vmem, vmem),
        scratch_shapes=[
            pltpu.VMEM((tokens * model // LANES, LANES), f32),
            pltpu.VMEM((tokens, LANES), f32),
        ],
        name="combine",
    )(target, back, gates)


def dot(a, b, ca, cb):
    return lax.dot_general(a, b, (((ca,), (cb,)), ((), ())), preferred_element_type=f32)


def experts_kernel(rows_hbm, *refs):
    blocks, stores_to, back_ref = refs[:10], refs[10:18], refs[18]
    rows, ins, outs, grads, total, lines, in_sems, out_sems = refs[19:]
    hidden, model = outs.shape[1], outs.shape[2]
    slots, width = rows.shape[0], model // LANES
    experts = slots // 2
    loads = [pltpu.make_async_copy(rows_hbm, rows, in_sems.at[0])]
    places = []
    for q in range(4):
        places.append((q, ins.at[q]))
        if q < 2:
            places.append((q, outs.at[q]))
        else:
            ahead, behind = pl.ds(0, AHEAD_OUT), pl.ds(AHEAD_OUT, hidden - AHEAD_OUT)
            places += [(q, outs.at[q, ahead, :]), (q, outs.at[q, behind, :])]
    loads += [
        pltpu.make_async_copy(block, place, in_sems.at[1 + n])
        for n, (block, (_, place)) in enumerate(zip(blocks, places))
    ]
    stores = []
    for q in range(4):
        cut = hidden if q < 2 else hidden + AHEAD_GRAD
        first = pltpu.make_async_copy(grads.at[q, pl.ds(0, cut), :], stores_to[2 * q], out_sems.at[2 * q])
        second = pltpu.make_async_copy(
            grads.at[q, pl.ds(cut, 2 * hidden - cut), :], stores_to[2 * q + 1], out_sems.at[2 * q + 1]
        )
        stores += [first, second]
    for load in loads:
        load.start()
    loads[0].wait()
    gate = jnp.zeros((slots, 1), f32)
    for q in range(4):
        for load, (user, _) in zip(loads[1:], places):
            if user == q:
                load.wait()
        preact = dot(rows[:, :model], ins[q], 1, 0)
        pulled = dot(rows[:, model:], outs[q], 1, 1)
        sig = jax.nn.sigmoid(preact)
        act = preact * sig
        d_pre = (pulled * sig * (1.0 + preact * (1.0 - sig))).astype(bf16)
        gate += jnp.sum(act * pulled, axis=1, keepdims=True)
        act = act.astype(bf16)
        grads[q, :hidden, :] = dot(d_pre, rows[:, :model], 0, 0).astype(bf16)
        grads[q, hidden:, :] = dot(act, rows[:, model:], 0, 0).astype(bf16)
        stores[2 * q].start()
        stores[2 * q + 1].start()
        part = dot(d_pre, ins[q], 1, 1)
        total[...] = part if q == 0 else total[...] + part
    for j in range(width):
        lines[pl.ds(j, slots, stride=width), :] = total[:, j * LANES : (j + 1) * LANES]
    back_ref[:, : 2 * width, :] = lines[...].astype(bf16).reshape(experts, 2 * width, LANES)
    gate = jnp.broadcast_to(gate, (slots, LANES))
    high = gate.astype(bf16)
    low = (gate - high.astype(f32)).astype(bf16)
    row = lax.broadcasted_iota(jnp.int32, (experts * GATE_ROWS, slots), 0)
    slot = lax.broadcasted_iota(jnp.int32, (experts * GATE_ROWS, slots), 1)
    place = row - (slot >> 1) * GATE_ROWS - 2 * (slot & 1)
    spread = dot((place == 0).astype(bf16), high, 1, 0) + dot((place == 1).astype(bf16), low, 1, 0)
    back_ref[:, 2 * width :, :] = spread.astype(bf16).reshape(experts, GATE_ROWS, LANES)
    for store in stores:
        store.wait()


def run_experts(rows, blocks):
    slots, model = rows.shape[0], rows.shape[1] // 2
    hidden = blocks[1].shape[0]
    width = model // LANES
    anywhere = pl.BlockSpec(memory_space=pl.ANY)
    vmem = pl.BlockSpec(memory_space=pltpu.VMEM)
    return pl.pallas_call(
        experts_kernel,
        out_shape=tuple(
            jax.ShapeDtypeStruct((r, model), bf16)
            for r in [hidden] * 4 + [hidden + AHEAD_GRAD, hidden - AHEAD_GRAD] * 2
        )
        + (jax.ShapeDtypeStruct((slots // 2, 2 * width + GATE_ROWS, LANES), bf16),),
        in_specs=[anywhere] * 11,
        out_specs=(anywhere,) * 8 + (vmem,),
        scratch_shapes=[
            pltpu.VMEM(rows.shape, bf16),
            pltpu.VMEM((4, model, hidden), bf16),
            pltpu.VMEM((4, hidden, model), bf16),
            pltpu.VMEM((4, 2 * hidden, model), bf16),
            pltpu.VMEM((slots, model), f32),
            pltpu.VMEM((slots * width, LANES), f32),
            pltpu.SemaphoreType.DMA((11,)),
            pltpu.SemaphoreType.DMA((8,)),
        ],
        cost_estimate=pl.CostEstimate(
            flops=4 * 5 * 2 * slots * model * hidden,
            bytes_accessed=2 * (rows.size + 16 * hidden * model),
            transcendentals=0,
        ),
        name="experts",
    )(rows, *blocks)


def finish_first_kernel(own_ref, peer_ref, came_ref, out_ref):
    total = own_ref[...].astype(f32) + peer_ref[...].astype(f32) + came_ref[...].astype(f32)
    out_ref[...] = total.T.astype(bf16)


def finish_second_kernel(own_ref, peer_ref, upper_ref, lower_ref, out_ref):
    half = upper_ref.shape[0]
    total = own_ref[...].astype(f32) + peer_ref[...].astype(f32)
    out_ref[:half, :] = (total[:half, :] + upper_ref[...].astype(f32)).astype(bf16)
    out_ref[half:, :] = (total[half:, :] + lower_ref[...].astype(f32)).astype(bf16)


def finish_first(own, peer, came):
    hidden, model = own.shape
    part = pl.BlockSpec((hidden, 512), lambda j: (0, j))
    return pl.pallas_call(
        finish_first_kernel,
        grid=(model // 512,),
        out_shape=jax.ShapeDtypeStruct((model, hidden), bf16),
        in_specs=[part] * 3,
        out_specs=pl.BlockSpec((512, hidden), lambda j: (j, 0)),
        name="finish_first",
    )(own, peer, came)


def finish_second(own, peer, came, rest):
    hidden, model = own.shape
    part = pl.BlockSpec((hidden, 1024), lambda j: (0, j))
    return pl.pallas_call(
        finish_second_kernel,
        grid=(model // 1024,),
        out_shape=jax.ShapeDtypeStruct((hidden, model), bf16),
        in_specs=[
            part,
            part,
            pl.BlockSpec((AHEAD_GRAD, 1024), lambda j: (hidden // AHEAD_GRAD, j)),
            pl.BlockSpec((hidden - AHEAD_GRAD, 1024), lambda j: (0, j)),
        ],
        out_specs=part,
        name="finish_second",
    )(own, peer, came, rest)


def exchange(x, groups):
    return lax.all_to_all(
        x, AXES, split_axis=0, concat_axis=0, axis_index_groups=groups, tiled=True
    )


def on_device(groups, tokens, d_out, expert_ids, gate_weights, w_in, w_out):
    tok_rows, model = tokens.shape
    width = model // LANES
    experts = len(groups[0])
    slots = 2 * experts
    own_in, own_out = w_in[0], w_out[0]
    gates = gate_weights.T
    oth_in = hold(lax.ppermute(own_in, "yl", SWAP), HOLD_FLOPS)
    oth_upper = hold(lax.ppermute(own_out[:AHEAD_OUT], "yl", SWAP), HOLD_FLOPS)
    outgoing, target = dispatch(expert_ids.T, gates, tokens, d_out, experts)
    arrived = exchange(outgoing.reshape(experts, 4 * width, LANES), groups)
    own_in, own_out, oth_in = lax.optimization_barrier((own_in, own_out, oth_in))
    oth_lower = hold(lax.ppermute(own_out[AHEAD_OUT:], "yl", SWAP), HOLD_FLOPS)
    near = [own_in, own_out, lax.ppermute(own_in, "core", SWAP), lax.ppermute(own_out, "core", SWAP)]
    far = [oth_in, oth_upper, oth_lower]
    far += [lax.ppermute(w, "core", SWAP) for w in far]
    arrived, *blocks = lax.optimization_barrier((arrived, *near, *far))
    rows = arrived.reshape(slots, 2 * model)
    own_gi, own_go, peer_gi, peer_go, far_a, far_b, send_a, send_b, back = run_experts(rows, blocks)

    def add(a, b):
        return (a.astype(f32) + b.astype(f32)).astype(bf16)

    sum_a = add(far_a, lax.ppermute(send_a, "core", SWAP))
    came_a = hold(lax.ppermute(sum_a, "yl", SWAP), HOLD_FLOPS)
    back, send_b, _ = lax.optimization_barrier((back, send_b, sum_a))
    returned = exchange(back, groups)
    got_b = hold(lax.ppermute(send_b, "core", SWAP), HOLD_FLOPS)
    sum_b = add(far_b, got_b)
    sum_b, peer_gi, peer_go = lax.optimization_barrier((sum_b, peer_gi, peer_go))
    came_b = lax.ppermute(sum_b, "yl", SWAP)
    near_in = lax.ppermute(peer_gi, "core", SWAP)
    near_out = lax.ppermute(peer_go, "core", SWAP)
    d_first = finish_first(own_gi, near_in, came_a)
    d_second = finish_second(own_go, near_out, came_a, came_b)
    returned, d_first, d_second = lax.optimization_barrier((returned, d_first, d_second))
    d_tokens, d_gates = combine(target, returned, gates, model)
    return (d_tokens, d_gates.T, d_first[None], d_second[None])


def solution(mesh):
    dp, expert = mesh.devices.shape
    pairs = expert // 4
    fine = Mesh(np.asarray(mesh.devices).reshape(dp, pairs, 2, 2), AXES)
    number = np.arange(dp * expert).reshape(dp, pairs, 2, 2)
    near = np.arange(pairs) >= pairs // 2
    groups = [
        [int(number[i, k, int(near[k]) ^ side, c]) for i in range(dp) for k in range(pairs)]
        for side in range(2)
        for c in range(2)
    ]
    flat, block = P(AXES, None), P(AXES, None, None)
    return jax.shard_map(
        functools.partial(on_device, groups),
        mesh=fine,
        in_specs=(flat, flat, flat, flat, block, block),
        out_specs=(flat, flat, block, block),
        check_vma=False,
    )
```
